32 devices in a mesh: fsdp: 16 (over z, y, x), seq: 2 (over core).
Axes of the slice: x: 2, y: 2, z: 4, core: 2. Of those that a mesh axis runs over, the one named last changes fastest.
Arguments:
- tokens: bfloat16 [24576, 1024], P(('fsdp', 'seq')), may hold values from -6 to 6
- cotangent: bfloat16 [24576, 1024], P(('fsdp', 'seq')), may hold values from -6 to 6
- lengths: int32 [16], P('fsdp'), may hold values from 768 to 1536, as said below
- master_in: float32 [1024, 3352], P(('fsdp', 'seq')), may hold values from -0.1875 to 0.1875
- master_qkv: float32 [1024, 768], P(('fsdp', 'seq')), may hold values from -0.1875 to 0.1875
- master_ssm_out: float32 [1536, 1024], P(('fsdp', 'seq')), may hold values from -0.15625 to 0.15625
- master_att_out: float32 [512, 1024], P(('fsdp', 'seq')), may hold values from -1 to 1
- master_gu: float32 [1024, 4096], P(('fsdp', 'seq')), may hold values from -0.1875 to 0.1875
- master_down: float32 [2048, 1024], P(('fsdp', 'seq')), may hold values from -0.125 to 0.125
- master_small: float32 [12616], replicated, may hold values from -7 to 5, as said below
- moment_in: float32 [1024, 3352], P(('fsdp', 'seq')), may hold values from -0.00018310547 to 0.00018310547
- moment_qkv: float32 [1024, 768], P(('fsdp', 'seq')), may hold values from -0.00018310547 to 0.00018310547
- moment_ssm_out: float32 [1536, 1024], P(('fsdp', 'seq')), may hold values from -0.00018310547 to 0.00018310547
- moment_att_out: float32 [512, 1024], P(('fsdp', 'seq')), may hold values from -0.00018310547 to 0.00018310547
- moment_gu: float32 [1024, 4096], P(('fsdp', 'seq')), may hold values from -0.00018310547 to 0.00018310547
- moment_down: float32 [2048, 1024], P(('fsdp', 'seq')), may hold values from -0.00018310547 to 0.00018310547
- moment_small: float32 [12616], replicated, may hold values from -0.00018310547 to 0.00018310547
- square_in: float32 [1024, 3352], P(('fsdp', 'seq')), may hold values from 2e-11 to 3e-10
- square_qkv: float32 [1024, 768], P(('fsdp', 'seq')), may hold values from 2e-11 to 3e-10
- square_ssm_out: float32 [1536, 1024], P(('fsdp', 'seq')), may hold values from 2e-11 to 3e-10
- square_att_out: float32 [512, 1024], P(('fsdp', 'seq')), may hold values from 2e-11 to 3e-10
- square_gu: float32 [1024, 4096], P(('fsdp', 'seq')), may hold values from 2e-11 to 3e-10
- square_down: float32 [2048, 1024], P(('fsdp', 'seq')), may hold values from 2e-11 to 3e-10
- square_small: float32 [12616], replicated, may hold values from 2e-11 to 3e-10
Outputs:
- output: bfloat16 [24576, 1024], P(('fsdp', 'seq'))
- token_grad: float32 [24576, 1024], P(('fsdp', 'seq'))
- grad_norm: float32 [], replicated
- grad_in: float32 [1024, 3352], P(('fsdp', 'seq'))
- grad_qkv: float32 [1024, 768], P(('fsdp', 'seq'))
- grad_ssm_out: float32 [1536, 1024], P(('fsdp', 'seq'))
- grad_att_out: float32 [512, 1024], P(('fsdp', 'seq'))
- grad_gu: float32 [1024, 4096], P(('fsdp', 'seq'))
- grad_down: float32 [2048, 1024], P(('fsdp', 'seq'))
- grad_small: float32 [12616], replicated
- new_in: float32 [1024, 3352], P(('fsdp', 'seq'))
- new_qkv: float32 [1024, 768], P(('fsdp', 'seq'))
- new_ssm_out: float32 [1536, 1024], P(('fsdp', 'seq'))
- new_att_out: float32 [512, 1024], P(('fsdp', 'seq'))
- new_gu: float32 [1024, 4096], P(('fsdp', 'seq'))
- new_down: float32 [2048, 1024], P(('fsdp', 'seq'))
- update_small: float32 [12616], replicated
- new_moment_in: float32 [1024, 3352], P(('fsdp', 'seq'))
- new_moment_qkv: float32 [1024, 768], P(('fsdp', 'seq'))
- new_moment_ssm_out: float32 [1536, 1024], P(('fsdp', 'seq'))
- new_moment_att_out: float32 [512, 1024], P(('fsdp', 'seq'))
- new_moment_gu: float32 [1024, 4096], P(('fsdp', 'seq'))
- new_moment_down: float32 [2048, 1024], P(('fsdp', 'seq'))
- new_moment_small: float32 [12616], replicated
- new_square_in: float32 [1024, 3352], P(('fsdp', 'seq'))
- new_square_qkv: float32 [1024, 768], P(('fsdp', 'seq'))
- new_square_ssm_out: float32 [1536, 1024], P(('fsdp', 'seq'))
- new_square_att_out: float32 [512, 1024], P(('fsdp', 'seq'))
- new_square_gu: float32 [1024, 4096], P(('fsdp', 'seq'))
- new_square_down: float32 [2048, 1024], P(('fsdp', 'seq'))
- new_square_small: float32 [12616], replicated
The draws below stay inside these ranges and needn't reach their ends.
Inputs may be any that keep to these rules, and one draw needn't show every extreme that they name: Positions 0 to lengths[f] - 1 of slot f are real, the rest padding; in every draw some slot is full. The pieces of master_small as listed in the first step.
All inputs are finite; a program needn't handle non-finite values.
Results may differ from the reference program's by a relative error of at most 0.015.
The reference program's roundings to bfloat16 on the way count: a program that leaves them out, or rounds other values in their place, can miss the bound.
Values may be sent and summed in bfloat16 or wider, within the bound.
No kernel may reach another device: no remote copies, remote signals or barrier semaphores. Data moves between devices by JAX's collectives and lax.ppermute only.
A program may use at most 320 MiB of HBM per device.

```python
import math
import jax
import jax.numpy as jnp
from jax import lax

D = 1024
FF = 2048
NHM = 24
HDM = 64
NSTATE = 128
HQ = 8
HK = 2
HD = 64
KCONV = 4
BLOCK_LEN = 128
QUERY_BLOCK = 512
STEP = 10
DSSM = 1536
CONVW = 1792
IN_W = 3352
QKV_W = 768
ATT_W = 512
NSMALL = 12616
SLOT = 1536
TOKENS = 24576
N_FSDP = 16
N_SEQ = 2


def draw_lengths(key, part):
    drawn = jax.random.randint(key, (N_FSDP,), SLOT // 2, SLOT + 1, dtype=jnp.int32)
    chosen = jax.random.randint(jax.random.fold_in(key, 7), (), 0, N_FSDP, dtype=jnp.int32)
    return jnp.where(jnp.arange(N_FSDP, dtype=jnp.int32) == chosen, SLOT, drawn).astype(jnp.int32)


def rising_gain(key, count):
    low_end = 0.5
    high_end = 2.0
    fraction = jnp.arange(count, dtype=jnp.float32) / (count - 1.0)
    ramp = jnp.exp(math.log(low_end) + (math.log(high_end) - math.log(low_end)) * fraction)
    return ramp * jax.random.uniform(key, (count,), jnp.float32, 0.8, 1.2)


def draw_master_small(key, part):
    subkeys = jax.random.split(key, 8)
    gain_in = rising_gain(subkeys[0], D)
    gain_ff = rising_gain(subkeys[6], D)
    gain_ssm = rising_gain(subkeys[7], DSSM)
    conv_bias = jax.random.uniform(subkeys[1], (CONVW,), jnp.float32, -0.5, 0.5)
    conv_flat = jax.random.uniform(subkeys[2], (KCONV * CONVW,), jnp.float32, -1.0, 1.0)
    step_init = jnp.exp(jax.random.uniform(subkeys[3], (NHM,), jnp.float32, math.log(0.001), math.log(0.1)))
    dt_bias = step_init + jnp.log(-jnp.expm1(-step_init))
    a_log = jnp.log(jax.random.uniform(subkeys[4], (NHM,), jnp.float32, 1.0, 16.0))
    d_skip = jax.random.uniform(subkeys[5], (NHM,), jnp.float32, 0.5, 1.5)
    return jnp.concatenate([gain_in, gain_ff, gain_ssm, conv_bias, conv_flat, dt_bias, a_log, d_skip]).astype(jnp.float32)


def block_levels(stream_key, extent, cuts, least, largest):
    factor_of, own = 1.0, jax.random.fold_in(stream_key, 6)
    for position, shards_of in cuts:
        heights = jnp.exp(jax.random.uniform(jax.random.fold_in(own, position), (shards_of,), jnp.float32, least / len(cuts), largest / len(cuts)))
        factor_of = factor_of * jnp.repeat(heights, extent[position] // shards_of).reshape([-1 if axis == position else 1 for axis in range(len(extent))])
    return factor_of


def gaussian(key, dims, deviation, bound, cuts=(), kind=jnp.bfloat16):
    values = deviation * jax.random.normal(key, dims, jnp.float32)
    if cuts:
        values = values * block_levels(key, dims, cuts, -0.22, 0.18)
    return jnp.clip(values, -bound, bound).astype(kind)


def setup_inputs(seed: int = 0) -> dict:
    seeds = jax.random.split(jax.random.key(seed), 25)
    tokens = gaussian(seeds[0], (TOKENS, D), 1.0, 6.0, ((0, 32),))
    cotangent = gaussian(seeds[1], (TOKENS, D), 1.0, 6.0, ((0, 32),))
    lengths = draw_lengths(jax.random.fold_in(seeds[24], 71), 0)
    master_in = gaussian(seeds[3], (D, IN_W), D ** -0.5, 0.1875, ((0, 32),), jnp.float32)
    master_qkv = gaussian(seeds[4], (D, QKV_W), D ** -0.5, 0.1875, ((0, 32),), jnp.float32)
    master_ssm_out = gaussian(seeds[5], (DSSM, D), DSSM ** -0.5, 0.15625, ((0, 32),), jnp.float32)
    master_att_out = gaussian(seeds[6], (ATT_W, D), (ATT_W // 16) ** -0.5, 1.0, ((0, 32),), jnp.float32)
    master_gu = gaussian(seeds[7], (D, 2 * FF), D ** -0.5, 0.1875, ((0, 32),), jnp.float32)
    master_down = gaussian(seeds[8], (FF, D), FF ** -0.5, 0.125, ((0, 32),), jnp.float32)
    master_small = draw_master_small(jax.random.fold_in(seeds[24], 71), 0)
    moment_in = gaussian(seeds[10], (D, IN_W), 0.00003, 0.00018310547, ((0, 32),), jnp.float32)
    moment_qkv = gaussian(seeds[11], (D, QKV_W), 0.00003, 0.00018310547, ((0, 32),), jnp.float32)
    moment_ssm_out = gaussian(seeds[12], (DSSM, D), 0.00003, 0.00018310547, ((0, 32),), jnp.float32)
    moment_att_out = gaussian(seeds[13], (ATT_W, D), 0.00003, 0.00018310547, ((0, 32),), jnp.float32)
    moment_gu = gaussian(seeds[14], (D, 2 * FF), 0.00003, 0.00018310547, ((0, 32),), jnp.float32)
    moment_down = gaussian(seeds[15], (FF, D), 0.00003, 0.00018310547, ((0, 32),), jnp.float32)
    moment_small = gaussian(seeds[16], (NSMALL,), 0.00003, 0.00018310547, (), jnp.float32)
    square_in = jnp.clip(jnp.exp(math.log(2.999999970665357e-10) - 2.7080502 * jax.random.uniform(seeds[17], (D, IN_W), jnp.float32) ** block_levels(seeds[17], (D, IN_W), ((0, 32),), -0.2, 0.2)), 1.9999999920083944e-11, 2.999999970665357e-10)
    square_qkv = jnp.clip(jnp.exp(math.log(2.999999970665357e-10) - 2.7080502 * jax.random.uniform(seeds[18], (D, QKV_W), jnp.float32) ** block_levels(seeds[18], (D, QKV_W), ((0, 32),), -0.2, 0.2)), 1.9999999920083944e-11, 2.999999970665357e-10)
    square_ssm_out = jnp.clip(jnp.exp(math.log(2.999999970665357e-10) - 2.7080502 * jax.random.uniform(seeds[19], (DSSM, D), jnp.float32) ** block_levels(seeds[19], (DSSM, D), ((0, 32),), -0.2, 0.2)), 1.9999999920083944e-11, 2.999999970665357e-10)
    square_att_out = jnp.clip(jnp.exp(math.log(2.999999970665357e-10) - 2.7080502 * jax.random.uniform(seeds[20], (ATT_W, D), jnp.float32) ** block_levels(seeds[20], (ATT_W, D), ((0, 32),), -0.2, 0.2)), 1.9999999920083944e-11, 2.999999970665357e-10)
    square_gu = jnp.clip(jnp.exp(math.log(2.999999970665357e-10) - 2.7080502 * jax.random.uniform(seeds[21], (D, 2 * FF), jnp.float32) ** block_levels(seeds[21], (D, 2 * FF), ((0, 32),), -0.2, 0.2)), 1.9999999920083944e-11, 2.999999970665357e-10)
    square_down = jnp.clip(jnp.exp(math.log(2.999999970665357e-10) - 2.7080502 * jax.random.uniform(seeds[22], (FF, D), jnp.float32) ** block_levels(seeds[22], (FF, D), ((0, 32),), -0.2, 0.2)), 1.9999999920083944e-11, 2.999999970665357e-10)
    square_small = jnp.clip(jnp.exp(jax.random.uniform(seeds[23], (NSMALL,), jnp.float32, math.log(1.9999999920083944e-11), math.log(2.999999970665357e-10))), 1.9999999920083944e-11, 2.999999970665357e-10)
    return {"tokens": tokens, "cotangent": cotangent, "lengths": lengths, "master_in": master_in, "master_qkv": master_qkv, "master_ssm_out": master_ssm_out, "master_att_out": master_att_out, "master_gu": master_gu, "master_down": master_down, "master_small": master_small, "moment_in": moment_in, "moment_qkv": moment_qkv, "moment_ssm_out": moment_ssm_out, "moment_att_out": moment_att_out, "moment_gu": moment_gu, "moment_down": moment_down, "moment_small": moment_small, "square_in": square_in, "square_qkv": square_qkv, "square_ssm_out": square_ssm_out, "square_att_out": square_att_out, "square_gu": square_gu, "square_down": square_down, "square_small": square_small}


@jax.custom_vjp
def low(v):
    return lax.optimization_barrier(v.astype(jnp.bfloat16)).astype(jnp.float32)

@jax.custom_vjp
def low_back(v):
    return v

def low_keep(v):
    return (low(v), None)

def low_pass(kept, grad):
    return (grad,)

def back_keep(v):
    return (v, None)

def back_low(kept, grad):
    return (low(grad),)
low.defvjp(low_keep, low_pass)
low_back.defvjp(back_keep, back_low)
norm_eps = 1e-05
rope_base = 10000.0
beta_first = 0.9
beta_second = 0.999
adam_eps = 1e-08
learn_rate = 0.04
decay_rate = 0.1
clip_norm = 1.0
masked_score = -1e+30
highest = lax.Precision.HIGHEST

def matmul(left, right):
    return jnp.dot(left, right, precision=highest, preferred_element_type=jnp.float32)

def rms_scale(values):
    return lax.rsqrt(lax.optimization_barrier(jnp.mean(values * values, axis=-1, keepdims=True)) + norm_eps)

def split_small(vector):
    widths = [D, D, DSSM, CONVW, KCONV * CONVW, NHM, NHM, NHM]
    pieces = []
    offset = 0
    for piece_width in widths:
        pieces.append(vector[offset:offset + piece_width])
        offset = offset + piece_width
    gain_in, gain_ff, gain_ssm, conv_bias, conv_flat, dt_bias, a_log, d_skip = pieces
    return (gain_in, gain_ff, gain_ssm, conv_bias, conv_flat.reshape(KCONV, CONVW), dt_bias, a_log, d_skip)

def rope_tables(length):
    half_dim = HD // 2
    positions = jnp.arange(length, dtype=jnp.float32)
    frequency = rope_base ** (-jnp.arange(half_dim, dtype=jnp.float32) * 2.0 / HD)
    angles = positions[:, None] * frequency[None, :]
    cosine = jnp.concatenate([jnp.cos(angles), jnp.cos(angles)], axis=1)
    sine = jnp.concatenate([jnp.sin(angles), jnp.sin(angles)], axis=1)
    return (cosine, sine)

def rotate(values, cosine, sine):
    half_dim = HD // 2
    turned = jnp.concatenate([-values[..., half_dim:], values[..., :half_dim]], axis=-1)
    return values * cosine[:, None, :] + turned * sine[:, None, :]

def mamba_mix(conv_input, step_raw, conv_weight, conv_bias, dt_bias, a_log, d_skip):
    length = conv_input.shape[0]
    head_count = step_raw.shape[1]
    inner_width = head_count * HDM
    padded = jnp.concatenate([jnp.zeros((KCONV - 1, conv_input.shape[1]), jnp.float32), conv_input], axis=0)
    conv_out = jnp.zeros_like(conv_input) + conv_bias[None, :]
    for tap_idx in range(KCONV):
        conv_out = conv_out + conv_weight[tap_idx][None, :] * padded[tap_idx:tap_idx + length]
    activated = jax.nn.silu(conv_out)
    x_heads = activated[:, :inner_width].reshape(length, head_count, HDM)
    b_state = activated[:, inner_width:inner_width + NSTATE]
    c_state = activated[:, inner_width + NSTATE:]
    step_size = jax.nn.softplus(step_raw + dt_bias[None, :])
    log_decay = -jnp.exp(a_log)[None, :] * step_size
    blocks = length // BLOCK_LEN
    x_step = (x_heads * step_size[:, :, None]).reshape(blocks, BLOCK_LEN, head_count, HDM)
    b_block = b_state.reshape(blocks, BLOCK_LEN, NSTATE)
    c_block = c_state.reshape(blocks, BLOCK_LEN, NSTATE)
    cumulative = jnp.cumsum(log_decay.reshape(blocks, BLOCK_LEN, head_count), axis=1)
    by_head = jnp.transpose(cumulative, (0, 2, 1))
    positions = jnp.arange(BLOCK_LEN, dtype=jnp.int32)
    lower_tri = positions[:, None] >= positions[None, :]
    spread = by_head[:, :, :, None] - by_head[:, :, None, :]
    decay_mat = jnp.where(lower_tri, jnp.exp(jnp.where(lower_tri, spread, 0.0)), 0.0)
    cb_product = jnp.einsum('cin,cjn->cij', c_block, b_block, precision=highest)
    y_inner = jnp.einsum('chij,cjhp->cihp', decay_mat * cb_product[:, None], x_step, precision=highest)
    to_end = jnp.exp(cumulative[:, -1:, :] - cumulative)
    block_state = jnp.einsum('cjhp,cjn->chpn', x_step * to_end[:, :, :, None], b_block, precision=highest)
    block_decay = jnp.exp(cumulative[:, -1, :])

    def advance(carried, inputs_pair):
        return (carried * inputs_pair[0][:, None, None] + inputs_pair[1], carried)
    _, entering = lax.scan(advance, jnp.zeros((head_count, HDM, NSTATE), jnp.float32), (block_decay, block_state))
    y_outer = jnp.einsum('cin,chpn->cihp', c_block, entering, precision=highest) * jnp.exp(cumulative)[:, :, :, None]
    combined = (y_inner + y_outer).reshape(length, head_count, HDM) + d_skip[None, :, None] * x_heads
    return combined.reshape(length, inner_width)

def attend_group(q_rot, k_rot, v_low):
    length = q_rot.shape[0]
    key_pos = jnp.arange(length, dtype=jnp.int32)
    score_scale = HD ** (-0.5)

    def one_block(offset):
        q_block = lax.dynamic_slice_in_dim(q_rot, offset, QUERY_BLOCK, 0)
        raw_scores = jnp.einsum('qgd,kd->gqk', q_block, k_rot, precision=highest)
        scores = low_back(raw_scores * score_scale)
        query_pos = offset + jnp.arange(QUERY_BLOCK, dtype=jnp.int32)
        allowed = key_pos[None, :] <= query_pos[:, None]
        scores = jnp.where(allowed[None], scores, masked_score)
        weights_p = jax.nn.softmax(scores, axis=-1)
        return jnp.einsum('gqk,kd->qgd', low(weights_p), v_low, precision=highest)
    offsets = jnp.arange(length // QUERY_BLOCK, dtype=jnp.int32) * QUERY_BLOCK
    result = lax.map(jax.checkpoint(one_block), offsets)
    return result.reshape(length, -1)

def slot_forward(x_slot, keep_mask, params):
    w_in, w_qkv, w_ssm_out, w_att_out, w_gu, w_down, small_vec = params
    gain_in, gain_ff, gain_ssm, conv_bias, conv_weight, dt_bias, a_log, d_skip = split_small(small_vec)
    length = x_slot.shape[0]
    normed = low(x_slot * rms_scale(x_slot) * gain_in)
    project = matmul(normed, w_in)
    z_gate = low_back(project[:, :DSSM])
    x_sent = low(low_back(project[:, DSSM:2 * DSSM]))
    bc_grad = low_back(project[:, 2 * DSSM:2 * DSSM + 2 * NSTATE])
    dt_sent = low(low_back(project[:, 2 * DSSM + 2 * NSTATE:]))
    qkv_sent = low(low_back(matmul(normed, w_qkv)))
    cosine, sine = rope_tables(length)
    per_group = NHM // N_SEQ
    query_group = HQ // HK
    group_width = per_group * HDM
    ssm_parts = []
    att_parts = []
    for group_idx in range(N_SEQ):
        bc_copy = low(low_back(bc_grad))
        col_lo = group_idx * group_width
        col_hi = col_lo + group_width
        conv_input = jnp.concatenate([x_sent[:, col_lo:col_hi], bc_copy], axis=1)
        conv_cols = jnp.concatenate([conv_weight[:, col_lo:col_hi], conv_weight[:, DSSM:]], axis=1)
        bias_cols = jnp.concatenate([conv_bias[col_lo:col_hi], conv_bias[DSSM:]])
        head_lo = group_idx * per_group
        head_hi = head_lo + per_group
        y_group = mamba_mix(conv_input, dt_sent[:, head_lo:head_hi], conv_cols, bias_cols, dt_bias[head_lo:head_hi], a_log[head_lo:head_hi], d_skip[head_lo:head_hi])
        ssm_parts.append(low(low_back(y_group)))
        q_heads = qkv_sent[:, group_idx * query_group * HD:(group_idx + 1) * query_group * HD].reshape(length, query_group, HD)
        k_head = qkv_sent[:, (HQ + group_idx) * HD:(HQ + group_idx + 1) * HD].reshape(length, 1, HD)
        v_head = qkv_sent[:, (HQ + HK + group_idx) * HD:(HQ + HK + group_idx + 1) * HD]
        q_rot = low(rotate(q_heads, cosine, sine))
        k_rot = low(rotate(k_head, cosine, sine))[:, 0]
        att_parts.append(low(low_back(attend_group(q_rot, k_rot, v_head))))
    ssm_all = jnp.concatenate(ssm_parts, axis=1)
    att_all = jnp.concatenate(att_parts, axis=1)
    gated_ssm = ssm_all * jax.nn.silu(z_gate)
    ssm_norm = low(gated_ssm * rms_scale(gated_ssm) * gain_ssm)
    mixer_out = low_back(matmul(ssm_norm, w_ssm_out) + matmul(att_all, w_att_out))
    residual = x_slot + mixer_out
    ff_in = low(residual * rms_scale(residual) * gain_ff)
    gate_up = low_back(matmul(ff_in, w_gu))
    hidden = low(jax.nn.silu(gate_up[:, :FF]) * gate_up[:, FF:])
    branch = low_back(matmul(hidden, w_down))
    return (residual + branch) * keep_mask[:, None]

def adam_update(master, moment_one, second, gradient, factor):
    clipped = gradient * factor
    new_one = beta_first * moment_one + (1.0 - beta_first) * clipped
    new_second = beta_second * second + (1.0 - beta_second) * clipped * clipped
    one_hat = new_one / (1.0 - beta_first ** STEP)
    second_hat = new_second / (1.0 - beta_second ** STEP)
    new_master = master - learn_rate * (one_hat / (jnp.sqrt(second_hat) + adam_eps) + decay_rate * master)
    return (new_master, new_one, new_second)

def reference(tokens, cotangent, lengths, master_in, master_qkv, master_ssm_out, master_att_out, master_gu, master_down, master_small, moment_in, moment_qkv, moment_ssm_out, moment_att_out, moment_gu, moment_down, moment_small, square_in, square_qkv, square_ssm_out, square_att_out, square_gu, square_down, square_small):
    masters = (master_in, master_qkv, master_ssm_out, master_att_out, master_gu, master_down, master_small)
    moments = (moment_in, moment_qkv, moment_ssm_out, moment_att_out, moment_gu, moment_down, moment_small)
    squares = (square_in, square_qkv, square_ssm_out, square_att_out, square_gu, square_down, square_small)
    x_slots = tokens.astype(jnp.float32).reshape(N_FSDP, SLOT, D)
    positions = jnp.arange(SLOT, dtype=jnp.int32)
    keep_masks = (positions[None, :] < lengths[:, None]).astype(jnp.float32)

    def forward(x_all, params):
        rounded = tuple((low(w) for w in params[:6])) + (params[6],)
        run_slot = jax.checkpoint(lambda slot_pair: slot_forward(slot_pair[0], slot_pair[1], rounded))
        return lax.map(run_slot, (x_all, keep_masks))
    full, pullback = jax.vjp(forward, x_slots, masters)
    d_tokens, grads = pullback(cotangent.astype(jnp.float32).reshape(N_FSDP, SLOT, D))
    output = full.reshape(TOKENS, D).astype(jnp.bfloat16)
    token_grad = d_tokens.reshape(TOKENS, D)
    total = jnp.zeros((), jnp.float32)
    for gradient in grads:
        total = total + jnp.sum(gradient * gradient)
    grad_norm = jnp.sqrt(total)
    factor = jnp.minimum(1.0, clip_norm / (grad_norm + 1e-06))
    updated = [adam_update(masters[i], moments[i], squares[i], grads[i], factor) for i in range(7)]
    update_small = updated[6][0] - master_small
    return (output, token_grad, grad_norm, grads[0], grads[1], grads[2], grads[3], grads[4], grads[5], grads[6], updated[0][0], updated[1][0], updated[2][0], updated[3][0], updated[4][0], updated[5][0], update_small, updated[0][1], updated[1][1], updated[2][1], updated[3][1], updated[4][1], updated[5][1], updated[6][1], updated[0][2], updated[1][2], updated[2][2], updated[3][2], updated[4][2], updated[5][2], updated[6][2])
```

```python
import jax
import jax.numpy as jnp
from jax import lax
from jax.experimental import pallas as pl
from jax.experimental.pallas import tpu as pltpu

f32 = jnp.float32
b16 = jnp.bfloat16
BL = 128
HDM = 64
NSTATE = 128
HD = 64
KCONV = 4
NEG = -1e30


def dot_nn(a, b):
    return lax.dot_general(a, b, (((1,), (0,)), ((), ())), preferred_element_type=f32)


def dot_nt(a, b):
    return lax.dot_general(a, b, (((1,), (1,)), ((), ())), preferred_element_type=f32)


def dot_tn(a, b):
    return lax.dot_general(a, b, (((0,), (0,)), ((), ())), preferred_element_type=f32)


def dot_exact(a, b):
    return lax.dot_general(
        a, b, (((1,), (0,)), ((), ())), preferred_element_type=f32, precision=lax.Precision.HIGHEST
    )


def lane_iota(shape):
    return lax.broadcasted_iota(jnp.int32, shape, 1)


def spread_heads(cols, pairs):
    low_half = lane_iota((cols.shape[0], 128)) < HDM
    return jnp.concatenate(
        [
            jnp.where(low_half, cols[:, 2 * k : 2 * k + 1], cols[:, 2 * k + 1 : 2 * k + 2])
            for k in range(pairs)
        ],
        axis=1,
    )


def halves(pair):
    low_half = lane_iota(pair.shape) < HDM
    zero = jnp.zeros_like(pair)
    return jnp.where(low_half, pair, zero), jnp.where(low_half, zero, pair)


def conv_parts(x_ref, bc_ref, halo, cw_ref, cb_ref):
    u = jnp.concatenate([x_ref[...], bc_ref[...]], axis=1).astype(f32)
    ext = jnp.concatenate([halo, u], axis=0)
    pre = cb_ref[...] + jnp.zeros_like(u)
    for k in range(KCONV):
        pre = pre + cw_ref[k : k + 1, :] * ext[5 + k : 5 + k + BL]
    sig = 1.0 / (1.0 + jnp.exp(-pre))
    return u, ext, pre, sig


def step_parts(dt_ref, hp_ref):
    raw = dt_ref[...].astype(f32) + hp_ref[0:1, :]
    step = jnp.maximum(raw, 0.0) + jnp.log1p(jnp.exp(-jnp.abs(raw)))
    log_decay = hp_ref[1:2, :] * step
    row = lax.broadcasted_iota(jnp.int32, (BL, BL), 0)
    col = lax.broadcasted_iota(jnp.int32, (BL, BL), 1)
    tril = (row >= col).astype(f32)
    cum = dot_exact(tril, log_decay)
    return raw, step, log_decay, cum, row, col


def mamba_fwd_body(x_ref, bc_ref, dt_ref, cw_ref, cb_ref, hp_ref, dsk_ref, y_ref, hs_ref, state, halo):
    width = x_ref.shape[1]
    pairs = width // 128

    @pl.when(pl.program_id(0) == 0)
    def _():
        state[...] = jnp.zeros_like(state)
        halo[...] = jnp.zeros_like(halo)

    u, ext, pre, sig = conv_parts(x_ref, bc_ref, halo[...], cw_ref, cb_ref)
    halo[...] = u[BL - 8 :]
    act = pre * sig
    x = act[:, :width]
    b_low = act[:, width : width + NSTATE].astype(b16)
    c_low = act[:, width + NSTATE :].astype(b16)
    _, step, _, cum, row, col = step_parts(dt_ref, hp_ref)
    cum_t = cum.T
    keep = row >= col
    cb = dot_nt(c_low, b_low)
    ecum = spread_heads(jnp.exp(cum), pairs)
    to_end = spread_heads(jnp.exp(cum[BL - 1 : BL, :] - cum), pairs)
    xs = x * spread_heads(step, pairs)
    h_old = state[...]
    hs_ref[0] = h_old
    outer = dot_nn(c_low, h_old.astype(b16)) * ecum + dsk_ref[...] * x
    for k in range(pairs):
        mats = []
        for h in (2 * k, 2 * k + 1):
            diff = cum[:, h : h + 1] - cum_t[h : h + 1, :]
            mats.append((jnp.exp(jnp.where(keep, diff, NEG)) * cb).astype(b16))
        lo, hi = halves(xs[:, 128 * k : 128 * k + 128].astype(b16))
        inner = dot_nn(jnp.concatenate(mats, axis=1), jnp.concatenate([lo, hi], axis=0))
        y_ref[:, 128 * k : 128 * k + 128] = (
            inner + outer[:, 128 * k : 128 * k + 128]
        ).astype(y_ref.dtype)
    state[...] = h_old * ecum[BL - 1 : BL, :] + dot_tn(b_low, (xs * to_end).astype(b16))


def seg_sum(values, seg_ref):
    hi = values.astype(b16)
    lo = (values - hi.astype(f32)).astype(b16)
    return dot_nn(hi, seg_ref[...]) + dot_nn(lo, seg_ref[...])


def mamba_bwd_body(
    x_ref, bc_ref, dt_ref, xp_ref, bcp_ref, dy_ref, hs_ref, cw_ref, cb_ref, hp_ref, dsk_ref, seg_ref,
    dmix_ref, dcw_ref, dhp_ref, dsk_grad_ref,
    dstate, halo_next, wrow, wcol,
):
    width = x_ref.shape[1]
    pairs = width // 128
    idx = pl.program_id(0)
    count = pl.num_programs(0)

    @pl.when(idx == 0)
    def _():
        dstate[...] = jnp.zeros_like(dstate)
        halo_next[...] = jnp.zeros_like(halo_next)
        wrow[...] = jnp.zeros_like(wrow)
        wcol[...] = jnp.zeros_like(wcol)
        dcw_ref[...] = jnp.zeros_like(dcw_ref)
        dhp_ref[...] = jnp.zeros_like(dhp_ref)
        dsk_grad_ref[...] = jnp.zeros_like(dsk_grad_ref)

    prev = jnp.concatenate([xp_ref[...], bcp_ref[...]], axis=1).astype(f32)[8:]
    prev = jnp.where(idx == count - 1, 0.0, prev)
    u, ext, pre, sig = conv_parts(x_ref, bc_ref, prev, cw_ref, cb_ref)
    act = pre * sig
    x = act[:, :width]
    b_low = act[:, width : width + NSTATE].astype(b16)
    c_low = act[:, width + NSTATE :].astype(b16)
    raw, step, log_decay, cum, row, col = step_parts(dt_ref, hp_ref)
    cum_t = cum.T
    keep_t = row <= col
    gt = dot_nt(b_low, c_low)
    ecum = spread_heads(jnp.exp(cum), pairs)
    to_end = spread_heads(jnp.exp(cum[BL - 1 : BL, :] - cum), pairs)
    step_wide = spread_heads(step, pairs)
    xs = x * step_wide
    xs_low = xs.astype(b16)
    dy_low = dy_ref[...]
    dy = dy_low.astype(f32)
    h_old = hs_ref[0]
    h_low = h_old.astype(b16)
    dh = dstate[...]
    dh_low = dh.astype(b16)
    ch = dot_nn(c_low, h_low)
    bds = dot_nn(b_low, dh_low)
    edy = ecum * dy
    edy_low = edy.astype(b16)
    z = xs * to_end
    d_c = dot_nt(edy_low, h_low)
    d_b = dot_nt(z.astype(b16), dh_low)
    q2 = z * bds
    q1 = edy * ch
    d_gt = jnp.zeros((BL, BL), f32)
    inners = []
    for k in range(pairs):
        dy_halves = halves(dy_low[:, 128 * k : 128 * k + 128])
        xs_pair = xs_low[:, 128 * k : 128 * k + 128]
        mats = []
        for j, h in enumerate((2 * k, 2 * k + 1)):
            diff = cum_t[h : h + 1, :] - cum[:, h : h + 1]
            lt = jnp.exp(jnp.where(keep_t, diff, NEG))
            d_mt = dot_nt(xs_pair, dy_halves[j]) * lt
            d_gt = d_gt + d_mt
            wt = d_mt * gt
            wrow[h : h + 1, :] = jnp.sum(wt, axis=0, keepdims=True)
            wcol[:, h : h + 1] = jnp.sum(wt, axis=1, keepdims=True)
            mats.append((lt * gt).astype(b16))
        inners.append(
            dot_nn(jnp.concatenate(mats, axis=1), jnp.concatenate(list(dy_halves), axis=0))
        )
    d_gt_low = d_gt.astype(b16)
    d_b = d_b + dot_nn(d_gt_low, c_low)
    d_c = d_c + dot_tn(d_gt_low, b_low)
    dxs = jnp.concatenate(inners, axis=1) + to_end * bds
    tail = jnp.sum(q2, axis=0, keepdims=True) + ecum[BL - 1 : BL, :] * jnp.sum(
        dh * h_old, axis=0, keepdims=True
    )
    tail_heads = seg_sum(jnp.broadcast_to(tail, (8, width)), seg_ref)[0:1, :]
    d_cum = seg_sum(q1 - q2, seg_ref) + wrow[...].T - wcol[...]
    d_cum = d_cum + jnp.where(row == BL - 1, tail_heads, 0.0)
    d_ld = dot_exact((row <= col).astype(f32), d_cum)
    d_step = seg_sum(dxs * x, seg_ref) + hp_ref[1:2, :] * d_ld
    d_raw = d_step / (1.0 + jnp.exp(-raw))
    dmix_ref[:, width : width + 128] = d_raw.astype(b16)
    dhp_ref[0:1, :] += jnp.sum(d_raw, axis=0, keepdims=True)
    dhp_ref[1:2, :] += jnp.sum(d_ld * log_decay, axis=0, keepdims=True)
    dsk_grad_ref[0:1, :] += jnp.sum(dy * x, axis=0, keepdims=True)
    dstate[...] = dh * ecum[BL - 1 : BL, :] + dot_tn(c_low, edy_low)
    d_x = dxs * step_wide + dsk_ref[...] * dy
    d_act = jnp.concatenate([d_x, d_b, d_c], axis=1)
    d_pre = d_act * sig * (1.0 + pre * (1.0 - sig))
    for k in range(KCONV):
        dcw_ref[k : k + 1, :] += jnp.sum(d_pre * ext[5 + k : 5 + k + BL], axis=0, keepdims=True)
    dcw_ref[KCONV : KCONV + 1, :] += jnp.sum(d_pre, axis=0, keepdims=True)
    ext_next = jnp.concatenate([d_pre, halo_next[...]], axis=0)
    halo_next[...] = d_pre[:8]
    du = jnp.zeros_like(d_pre)
    for k in range(KCONV):
        du = du + cw_ref[k : k + 1, :] * ext_next[3 - k : 3 - k + BL]
    dmix_ref[:, :width] = du[:, :width].astype(b16)
    dmix_ref[:, width + 128 :] = du[:, width:].astype(b16)


def mamba_fwd(mixed, conv_w, conv_b, head_rows, skip_row, width):
    length = mixed.shape[0]
    blocks = length // BL
    full = lambda shape: pl.BlockSpec(shape, lambda i: (0,) * len(shape))
    return pl.pallas_call(
        mamba_fwd_body,
        grid=(blocks,),
        in_specs=[
            pl.BlockSpec((BL, width), lambda i: (i, 0)),
            pl.BlockSpec((BL, 2 * NSTATE), lambda i: (i, 5)),
            pl.BlockSpec((BL, 128), lambda i: (i, 9)),
            full(conv_w.shape),
            full(conv_b.shape),
            full(head_rows.shape),
            full(skip_row.shape),
        ],
        out_specs=[
            pl.BlockSpec((BL, width), lambda i: (i, 0)),
            pl.BlockSpec((1, NSTATE, width), lambda i: (i, 0, 0)),
        ],
        out_shape=[
            jax.ShapeDtypeStruct((length, width), b16),
            jax.ShapeDtypeStruct((blocks, NSTATE, width), f32),
        ],
        scratch_shapes=[pltpu.VMEM((NSTATE, width), f32), pltpu.VMEM((8, width + 2 * NSTATE), f32)],
        compiler_params=pltpu.CompilerParams(dimension_semantics=("arbitrary",)),
        name="mamba_fwd",
    )(mixed, mixed, mixed, conv_w, conv_b, head_rows, skip_row)


def mamba_bwd(mixed, d_y, states, conv_w, conv_b, head_rows, skip_row, seg, width):
    length = mixed.shape[0]
    blocks = length // BL
    full = lambda shape: pl.BlockSpec(shape, lambda i: (0,) * len(shape))
    last = blocks - 1
    per = BL // 16
    back = lambda j: (lambda i: (last - i, j))
    prior = lambda j: (lambda i: (jnp.maximum((last - i) * per - 1, 0), j))
    return pl.pallas_call(
        mamba_bwd_body,
        grid=(blocks,),
        in_specs=[
            pl.BlockSpec((BL, width), back(0)),
            pl.BlockSpec((BL, 2 * NSTATE), back(5)),
            pl.BlockSpec((BL, 128), back(9)),
            pl.BlockSpec((16, width), prior(0)),
            pl.BlockSpec((16, 2 * NSTATE), prior(5)),
            pl.BlockSpec((BL, width), back(0)),
            pl.BlockSpec((1, NSTATE, width), lambda i: (last - i, 0, 0)),
            full(conv_w.shape),
            full(conv_b.shape),
            full(head_rows.shape),
            full(skip_row.shape),
            full(seg.shape),
        ],
        out_specs=[
            pl.BlockSpec((BL, width + 128 + 2 * NSTATE), back(0)),
            full((8, width + 2 * NSTATE)),
            full((8, 128)),
            full((8, width)),
        ],
        out_shape=[
            jax.ShapeDtypeStruct((length, width + 128 + 2 * NSTATE), b16),
            jax.ShapeDtypeStruct((8, width + 2 * NSTATE), f32),
            jax.ShapeDtypeStruct((8, 128), f32),
            jax.ShapeDtypeStruct((8, width), f32),
        ],
        scratch_shapes=[
            pltpu.VMEM((NSTATE, width), f32),
            pltpu.VMEM((8, width + 2 * NSTATE), f32),
            pltpu.VMEM((BL, 128), f32),
            pltpu.VMEM((BL, 128), f32),
        ],
        compiler_params=pltpu.CompilerParams(dimension_semantics=("arbitrary",)),
        name="mamba_bwd",
    )(mixed, mixed, mixed, mixed, mixed, d_y, states, conv_w, conv_b, head_rows, skip_row, seg)


QB = 512


def turn(values, rot):
    return dot_nn(values, rot)


def rotated(att_ref, cos_ref, sin_ref, rot_ref, q_s, kk_s, vv_s, nq):
    cos = cos_ref[...]
    sin = sin_ref[...]
    rot = rot_ref[...]
    for p in range(nq):
        raw = att_ref[:, 128 * p : 128 * p + 128]
        q_s[:, 128 * p : 128 * p + 128] = (raw.astype(f32) * cos + turn(raw, rot) * sin).astype(b16)
    kv = att_ref[:, 128 * nq : 128 * nq + 128]
    low_half = lane_iota(kv.shape) < HD
    kv_wide = kv.astype(f32)
    kv_swap = pltpu.roll(kv_wide, HD, 1)
    kk = jnp.where(low_half, kv_wide, kv_swap).astype(b16)
    vv_s[...] = jnp.where(low_half, kv_swap, kv_wide).astype(b16)
    kk_s[...] = (kk.astype(f32) * cos + turn(kk, rot) * sin).astype(b16)


def attn_fwd_body(att_ref, cos_ref, sin_ref, rot_ref, o_ref, lse_ref, q_s, kk_s, vv_s):
    length = att_ref.shape[0]
    nq = o_ref.shape[1] // 128
    rotated(att_ref, cos_ref, sin_ref, rot_ref, q_s, kk_s, vv_s, nq)
    scale = HD ** (-0.5)
    for qi in range(length // QB):
        n = (qi + 1) * QB
        row = lax.broadcasted_iota(jnp.int32, (QB, QB), 0)
        col = lax.broadcasted_iota(jnp.int32, (QB, QB), 1)
        for p in range(nq):
            q_halves = halves(q_s[qi * QB : n, 128 * p : 128 * p + 128])
            v_halves = halves(vv_s[0:n, :])
            out = jnp.zeros((QB, 128), f32)
            for j in range(2):
                s = dot_nt(q_halves[j], kk_s[0:n, :]) * scale
                diag = jnp.where(row >= col, s[:, n - QB :], NEG)
                s = diag if qi == 0 else jnp.concatenate([s[:, : n - QB], diag], axis=1)
                top = jnp.max(s, axis=1, keepdims=True)
                e = jnp.exp(s - top)
                total = jnp.sum(e, axis=1, keepdims=True)
                w = (e * (1.0 / total)).astype(b16)
                out = out + dot_nn(w, v_halves[j])
                h = 2 * p + j
                lse_ref[qi * QB : n, h : h + 1] = top + jnp.log(total)
            o_ref[qi * QB : n, 128 * p : 128 * p + 128] = out.astype(o_ref.dtype)


def attn_bwd_body(
    att_ref, cos_ref, sin_ref, rot_ref, rot_t_ref, lse_ref, do_ref, d_ref, q_s, kk_s, vv_s, dk_s, dv_s
):
    length = att_ref.shape[0]
    nq = do_ref.shape[1] // 128
    rotated(att_ref, cos_ref, sin_ref, rot_ref, q_s, kk_s, vv_s, nq)
    scale = HD ** (-0.5)
    dk_s[...] = jnp.zeros_like(dk_s)
    dv_s[...] = jnp.zeros_like(dv_s)
    rot_t = rot_t_ref[...]
    kk_t = kk_s[...].astype(f32).T
    sub_low = lax.broadcasted_iota(jnp.int32, kk_t.shape, 0) < HD
    kt_halves = (
        jnp.where(sub_low, kk_t, 0.0).astype(b16),
        jnp.where(sub_low, 0.0, kk_t).astype(b16),
    )
    row = lax.broadcasted_iota(jnp.int32, (QB, QB), 0)
    col = lax.broadcasted_iota(jnp.int32, (QB, QB), 1)
    for qi in range(length // QB):
        rows = slice(qi * QB, (qi + 1) * QB)
        lse_t = lse_ref[rows, :].T
        for p in range(nq):
            q_halves = halves(q_s[rows, 128 * p : 128 * p + 128])
            do_halves = halves(do_ref[rows, 128 * p : 128 * p + 128])
            dq_t = jnp.zeros((128, QB), f32)
            for j in range(2):
                h = 2 * p + j
                weights = []
                d_weights = []
                dots = jnp.zeros((1, QB), f32)
                for kj in range(qi + 1):
                    keys = slice(kj * QB, (kj + 1) * QB)
                    s = dot_nt(kk_s[keys, :], q_halves[j]) * scale - lse_t[h : h + 1, :]
                    if kj == qi:
                        s = jnp.where(row <= col, s, NEG)
                    w = jnp.exp(s)
                    dw = dot_nt(vv_s[keys, :], do_halves[j])
                    dots = dots + jnp.sum(w * dw, axis=0, keepdims=True)
                    weights.append(w)
                    d_weights.append(dw)
                for kj in range(qi + 1):
                    keys = slice(kj * QB, (kj + 1) * QB)
                    ds = (weights[kj] * (d_weights[kj] - dots)).astype(b16)
                    dv_s[keys, :] += dot_nn(weights[kj].astype(b16), do_halves[j])
                    dk_s[keys, :] += dot_nn(ds, q_halves[j])
                    dq_t = dq_t + dot_nn(kt_halves[j][:, keys], ds)
            dq = dq_t.T * scale
            cos = cos_ref[rows, :]
            sin = sin_ref[rows, :]
            back = dq * cos + dot_exact(dq * sin, rot_t)
            d_ref[rows, 128 * p : 128 * p + 128] = back.astype(b16)
    low_half = lane_iota(dk_s.shape) < HD
    dk = dk_s[...] * scale
    dk = dk + pltpu.roll(dk, HD, 1)
    dv = dv_s[...]
    dv = dv + pltpu.roll(dv, HD, 1)
    dk = dk * cos_ref[...] + dot_exact(dk * sin_ref[...], rot_t)
    d_ref[:, 128 * nq : 128 * nq + 128] = jnp.where(low_half, dk, dv).astype(b16)


def rope_rows(length):
    half_dim = HD // 2
    positions = jnp.arange(length, dtype=f32)
    frequency = 10000.0 ** (-jnp.arange(half_dim, dtype=f32) * 2.0 / HD)
    angles = positions[:, None] * frequency[None, :]
    cosine = jnp.cos(angles)
    sine = jnp.sin(angles)
    return jnp.concatenate([cosine] * 4, axis=1), jnp.concatenate([sine] * 4, axis=1)


def turn_matrix():
    row = lax.broadcasted_iota(jnp.int32, (128, 128), 0)
    col = lax.broadcasted_iota(jnp.int32, (128, 128), 1)
    same = (row // HD) == (col // HD)
    plus = same & (col - row == HD // 2)
    minus = same & (row - col == HD // 2)
    return plus.astype(f32) - minus.astype(f32)


def attn_fwd(mixed, cos, sin, rot, q_width):
    length = mixed.shape[0]
    width = q_width + 128
    spec = lambda shape: pl.BlockSpec(shape, lambda i: (0,) * len(shape))
    return pl.pallas_call(
        attn_fwd_body,
        grid=(1,),
        in_specs=[
            pl.BlockSpec((length, width), lambda i: (0, 2)),
            spec((length, 128)),
            spec((length, 128)),
            spec((128, 128)),
        ],
        out_specs=[spec((length, q_width)), spec((length, 128))],
        out_shape=[
            jax.ShapeDtypeStruct((length, q_width), b16),
            jax.ShapeDtypeStruct((length, 128), f32),
        ],
        scratch_shapes=[
            pltpu.VMEM((length, q_width), b16),
            pltpu.VMEM((length, 128), b16),
            pltpu.VMEM((length, 128), b16),
        ],
        name="attn_fwd",
    )(mixed, cos, sin, rot.astype(b16))


def attn_bwd(mixed, cos, sin, rot, lse, d_out):
    length = mixed.shape[0]
    q_width = d_out.shape[1]
    width = q_width + 128
    spec = lambda shape: pl.BlockSpec(shape, lambda i: (0,) * len(shape))
    return pl.pallas_call(
        attn_bwd_body,
        grid=(1,),
        in_specs=[
            pl.BlockSpec((length, width), lambda i: (0, 2)),
            spec((length, 128)),
            spec((length, 128)),
            spec((128, 128)),
            spec((128, 128)),
            spec((length, 128)),
            spec((length, q_width)),
        ],
        out_specs=spec((length, width)),
        out_shape=jax.ShapeDtypeStruct((length, width), b16),
        scratch_shapes=[
            pltpu.VMEM((length, q_width), b16),
            pltpu.VMEM((length, 128), b16),
            pltpu.VMEM((length, 128), b16),
            pltpu.VMEM((length, 128), f32),
            pltpu.VMEM((length, 128), f32),
        ],
        name="attn_bwd",
    )(mixed, cos, sin, rot.astype(b16), rot.T, lse, d_out)


from jax.sharding import PartitionSpec as P

D = 1024
FF = 2048
NHM = 24
HQ = 8
HK = 2
STEP = 10
DSSM = 1536
CONVW = 1792
GX = DSSM // 2
GQ = HQ // 2 * HD
GCOLS = GX + GQ + 2 * HD + 128
GDT = GX + GQ + 2 * HD
BCW = 2 * NSTATE
RB = 256
CB = 256
PSEUDO = 32

norm_eps = 1e-05
beta_first = 0.9
beta_second = 0.999
adam_eps = 1e-08
learn_rate = 0.04
decay_rate = 0.1
clip_norm = 1.0
BOTH = ("fsdp", "seq")
SWAP = [(0, 1), (1, 0)]


def whole_spec(shape):
    return pl.BlockSpec(shape, lambda *_: (0,) * len(shape))


def held_spec(shape):
    return pl.BlockSpec(shape, lambda *_: (0,) * len(shape), pipeline_mode=pl.Buffered(1))


def split_small(vector):
    widths = [D, D, DSSM, CONVW, KCONV * CONVW, NHM, NHM, NHM]
    pieces = []
    offset = 0
    for piece_width in widths:
        pieces.append(vector[offset : offset + piece_width])
        offset = offset + piece_width
    gain_in, gain_ff, gain_ssm, conv_bias, conv_flat, dt_bias, a_log, d_skip = pieces
    return (
        gain_in,
        gain_ff,
        gain_ssm,
        conv_bias,
        conv_flat.reshape(KCONV, CONVW),
        dt_bias,
        a_log,
        d_skip,
    )


def send_body(n_ref, w0_ref, w1_ref, w2_ref, o_ref):
    g = pl.program_id(0)
    j = pl.program_id(1)
    last = pl.num_programs(1) - 1

    @pl.when((j < last) & (g == 0))
    def _():
        o_ref[0] = dot_nn(n_ref[...], w0_ref[...]).astype(b16)

    @pl.when((j < last) & (g == 1))
    def _():
        o_ref[0] = dot_nn(n_ref[...], w1_ref[...]).astype(b16)

    @pl.when(j == last)
    def _():
        o_ref[0] = dot_nn(n_ref[...], w2_ref[...]).astype(b16)


def project_send(normed, w0, w1, w2):
    rows = normed.shape[0]
    nb = GCOLS // CB
    return pl.pallas_call(
        send_body,
        grid=(2, nb + 1),
        in_specs=[
            whole_spec(normed.shape),
            pl.BlockSpec((D, CB), lambda g, j: (0, jnp.where(g == 0, jnp.minimum(j, nb - 1), nb - 1))),
            pl.BlockSpec((D, CB), lambda g, j: (0, jnp.where(g == 1, jnp.minimum(j, nb - 1), 0))),
            pl.BlockSpec((D, CB), lambda g, j: (0, 0)),
        ],
        out_specs=pl.BlockSpec((1, rows, CB), lambda g, j: (g, 0, j)),
        out_shape=jax.ShapeDtypeStruct((2, rows, GCOLS + BCW), b16),
        name="project_send",
    )(normed, w0, w1, w2)


def gate_body(n_ref, w_ref, o_ref):
    o_ref[...] = dot_nn(n_ref[...], w_ref[...])


def project_gate(normed, w2):
    rows = normed.shape[0]
    return pl.pallas_call(
        gate_body,
        grid=(DSSM // CB,),
        in_specs=[whole_spec(normed.shape), pl.BlockSpec((D, CB), lambda j: (0, j + 1))],
        out_specs=pl.BlockSpec((rows, CB), lambda j: (0, j)),
        out_shape=jax.ShapeDtypeStruct((rows, DSSM), f32),
        name="project_gate",
    )(normed, w2)


def norm_back(values, scaling, gain_vec, d_normed):
    weighted = d_normed * gain_vec
    gain_grad = jnp.sum(d_normed * values * scaling, axis=0, keepdims=True)
    d_values = scaling * weighted - values * scaling**3 * jnp.mean(
        weighted * values, axis=-1, keepdims=True
    )
    return gain_grad, d_values


def rms_scale(values):
    return lax.rsqrt(jnp.mean(values * values, axis=-1, keepdims=True) + norm_eps)


def middle_body(
    tok_ref, cot_ref, keep_ref, ys_ref, att_ref, z_ref, w_ref, gff_ref, gssm_ref,
    out_ref, dres_ref, norm_ref, ffin_ref, hid_ref, dgu_ref, dbr_ref, dmix_ref, dys_ref, datt_ref, dz_ref,
    ggff_ref, ggssm_ref,
    gate_s, up_s,
):
    @pl.when(pl.program_id(0) == 0)
    def _():
        ggff_ref[...] = jnp.zeros_like(ggff_ref)
        ggssm_ref[...] = jnp.zeros_like(ggssm_ref)

    def weight(first, rows, lo=0, hi=PSEUDO):
        return w_ref[lo:hi, first : first + rows, :].reshape((hi - lo) * rows, D)

    w_so = lambda: weight(0, 48)
    w_ao = lambda: weight(48, 16)
    w_down = lambda b: weight(64, 64, 16 * b, 16 * b + 16)
    w_gu = lambda b: weight(128 + 32 * b, 32)

    ys = jnp.concatenate([ys_ref[0], ys_ref[1]], axis=1).astype(f32)
    z = z_ref[...]
    sig_z = 1.0 / (1.0 + jnp.exp(-z))
    silu_z = z * sig_z
    gated = ys * silu_z
    scale_ssm = rms_scale(gated)
    gain_ssm = gssm_ref[...]
    ssm_norm = (gated * scale_ssm * gain_ssm).astype(b16)
    norm_ref[...] = ssm_norm
    att = jnp.concatenate([att_ref[0], att_ref[1]], axis=1)
    residual = tok_ref[...].astype(f32) + (dot_nn(ssm_norm, w_so()) + dot_nn(att, w_ao()))
    scale_ff = rms_scale(residual)
    gain_ff = gff_ref[...]
    ff_in = (residual * scale_ff * gain_ff).astype(b16)
    ffin_ref[...] = ff_in
    branch = jnp.zeros_like(residual)
    for b in range(2):
        gate = dot_nn(ff_in, w_gu(b))
        up = dot_nn(ff_in, w_gu(b + 2))
        gate_s[b] = gate
        up_s[b] = up
        hidden = (gate * (1.0 / (1.0 + jnp.exp(-gate))) * up).astype(b16)
        hid_ref[:, D * b : D * b + D] = hidden
        branch = branch + dot_nn(hidden, w_down(b))
    keep = keep_ref[...]
    out_ref[...] = ((residual + branch) * keep).astype(b16)
    d_out = cot_ref[...].astype(f32) * keep
    d_branch = d_out.astype(b16)
    dbr_ref[...] = d_branch
    d_ff_in = jnp.zeros_like(residual)
    for b in range(2):
        gate = gate_s[b]
        up = up_s[b]
        sig = 1.0 / (1.0 + jnp.exp(-gate))
        d_hidden = dot_nt(d_branch, w_down(b))
        d_gate = (d_hidden * up * sig * (1.0 + gate * (1.0 - sig))).astype(b16)
        d_up = (d_hidden * gate * sig).astype(b16)
        dgu_ref[:, D * b : D * b + D] = d_gate
        dgu_ref[:, FF + D * b : FF + D * b + D] = d_up
        d_ff_in = d_ff_in + dot_nt(d_gate, w_gu(b)) + dot_nt(d_up, w_gu(b + 2))
    gain_grad, d_norm = norm_back(residual, scale_ff, gain_ff, d_ff_in)
    ggff_ref[0:1, :] += gain_grad
    d_residual = d_out + d_norm
    dres_ref[...] = d_residual
    d_mixer = d_residual.astype(b16)
    dmix_ref[...] = d_mixer
    d_att = dot_nt(d_mixer, w_ao()).astype(b16)
    datt_ref[0] = d_att[:, :GQ]
    datt_ref[1] = d_att[:, GQ:]
    gain_grad, d_gated = norm_back(gated, scale_ssm, gain_ssm, dot_nt(d_mixer, w_so()))
    ggssm_ref[0:1, :] += gain_grad
    d_ys = (d_gated * silu_z).astype(b16)
    dys_ref[0] = d_ys[:, :GX]
    dys_ref[1] = d_ys[:, GX:]
    dz_ref[...] = (d_gated * ys * sig_z * (1.0 + z * (1.0 - sig_z))).astype(b16)


def middle(tokens, cotangent, keep, ys, att, z, weights, gain_ff, gain_ssm):
    rows = tokens.shape[0]
    row = lambda width: pl.BlockSpec((RB, width), lambda i: (i, 0))
    pair = lambda width: pl.BlockSpec((2, RB, width), lambda i: (0, i, 0))
    sds = jax.ShapeDtypeStruct
    return pl.pallas_call(
        middle_body,
        grid=(rows // RB,),
        in_specs=[
            row(D), row(D), row(1), pair(GX), pair(GQ), row(DSSM),
            held_spec(weights.shape), whole_spec((1, D)), whole_spec((1, DSSM)),
        ],
        out_specs=[
            row(D), row(D), row(DSSM), row(D), row(FF), row(2 * FF), row(D), row(D),
            pair(GX), pair(GQ), row(DSSM), whole_spec((8, D)), whole_spec((8, DSSM)),
        ],
        out_shape=[
            sds((rows, D), b16), sds((rows, D), f32), sds((rows, DSSM), b16), sds((rows, D), b16),
            sds((rows, FF), b16), sds((rows, 2 * FF), b16), sds((rows, D), b16), sds((rows, D), b16),
            sds((2, rows, GX), b16), sds((2, rows, GQ), b16), sds((rows, DSSM), b16),
            sds((8, D), f32), sds((8, DSSM), f32),
        ],
        scratch_shapes=[pltpu.VMEM((2, RB, D), f32), pltpu.VMEM((2, RB, D), f32)],
        compiler_params=pltpu.CompilerParams(vmem_limit_bytes=60 * 1024 * 1024),
        name="middle",
    )(tokens, cotangent, keep, ys, att, z, weights, gain_ff, gain_ssm)


def flip(values):
    return values.astype(f32).T.astype(b16)


def grads_body(
    ffin_ref, hid_ref, norm_ref, att_ref, g0_ref, g1_ref, g2_ref, g3_ref, dbr_ref, dmix_ref,
    o_ref, ffin_t, hid_t, norm_t, att_t,
):
    @pl.when(pl.program_id(0) == 0)
    def _():
        ffin_t[...] = flip(ffin_ref[...])
        hid_t[...] = flip(hid_ref[...])
        norm_t[...] = flip(norm_ref[...])
        att_t[:GQ, :] = flip(att_ref[0])
        att_t[GQ:, :] = flip(att_ref[1])

    def put(first, rows, value):
        o_ref[:, first : first + rows, :] = value.astype(b16).reshape(PSEUDO, rows, CB)

    put(0, 48, dot_nn(norm_t[...], dmix_ref[...]))
    put(48, 16, dot_nn(att_t[...], dmix_ref[...]))
    put(64, 64, dot_nn(hid_t[...], dbr_ref[...]))
    for b, g_ref in enumerate((g0_ref, g1_ref, g2_ref, g3_ref)):
        put(128 + 32 * b, 32, dot_nn(ffin_t[...], g_ref[...]))


def middle_grads(ff_in, hidden, ssm_norm, att, d_gate_up, d_branch, d_mixer):
    rows = ff_in.shape[0]
    nb = D // CB
    col = lambda first: pl.BlockSpec((rows, CB), lambda j: (0, first + j))
    return pl.pallas_call(
        grads_body,
        grid=(nb,),
        in_specs=[
            held_spec(ff_in.shape), held_spec(hidden.shape), held_spec(ssm_norm.shape), held_spec(att.shape),
            col(0), col(nb), col(2 * nb), col(3 * nb), col(0), col(0),
        ],
        out_specs=pl.BlockSpec((PSEUDO, 256, CB), lambda j: (0, 0, j)),
        out_shape=jax.ShapeDtypeStruct((PSEUDO, 256, D), b16),
        scratch_shapes=[
            pltpu.VMEM((D, rows), b16), pltpu.VMEM((FF, rows), b16),
            pltpu.VMEM((DSSM, rows), b16), pltpu.VMEM((2 * GQ, rows), b16),
        ],
        compiler_params=pltpu.CompilerParams(vmem_limit_bytes=60 * 1024 * 1024),
        name="middle_grads",
    )(ff_in, hidden, ssm_norm, att, d_gate_up, d_gate_up, d_gate_up, d_gate_up, d_branch, d_mixer)


def entry_body(tok_ref, dres_ref, dm_ref, da_ref, dz_ref, w0_ref, w1_ref, w2_ref, gin_ref,
               tg_ref, p0_ref, p1_ref, p2_ref, gg_ref):
    @pl.when(pl.program_id(0) == 0)
    def _():
        gg_ref[...] = jnp.zeros_like(gg_ref)

    def group(g):
        return jnp.concatenate(
            [dm_ref[g][:, :GX], da_ref[g], dm_ref[g][:, GX : GX + 128]], axis=1
        )

    p0 = group(0)
    p1 = group(1)
    d_bc = (dm_ref[0][:, GX + 128 :].astype(f32) + dm_ref[1][:, GX + 128 :].astype(f32)).astype(b16)
    p2 = jnp.concatenate([d_bc, dz_ref[...]], axis=1)
    p0_ref[...] = p0
    p1_ref[...] = p1
    p2_ref[...] = p2
    d_normed = dot_nt(p0, w0_ref[...]) + dot_nt(p1, w1_ref[...]) + dot_nt(p2, w2_ref[...])
    x = tok_ref[...].astype(f32)
    gain_grad, d_x = norm_back(x, rms_scale(x), gin_ref[...], d_normed)
    gg_ref[0:1, :] += gain_grad
    tg_ref[...] = dres_ref[...] + d_x


def entry_back(tokens, d_residual, d_mix, d_att, d_z, w0, w1, w2, gain_in):
    rows = tokens.shape[0]
    row = lambda width: pl.BlockSpec((RB, width), lambda i: (i, 0))
    pair = lambda width: pl.BlockSpec((2, RB, width), lambda i: (0, i, 0))
    sds = jax.ShapeDtypeStruct
    return pl.pallas_call(
        entry_body,
        grid=(rows // RB,),
        in_specs=[
            row(D), row(D), pair(d_mix.shape[2]), pair(d_att.shape[2]), row(DSSM),
            held_spec(w0.shape), held_spec(w1.shape), held_spec(w2.shape), whole_spec((1, D)),
        ],
        out_specs=[row(D), row(w0.shape[1]), row(w1.shape[1]), row(w2.shape[1]), whole_spec((8, D))],
        out_shape=[
            sds((rows, D), f32), sds((rows, w0.shape[1]), b16), sds((rows, w1.shape[1]), b16),
            sds((rows, w2.shape[1]), b16), sds((8, D), f32),
        ],
        compiler_params=pltpu.CompilerParams(vmem_limit_bytes=60 * 1024 * 1024),
        name="entry_back",
    )(tokens, d_residual, d_mix, d_att, d_z, w0, w1, w2, gain_in)


def entry_grad_body(nt_ref, p_ref, o_ref):
    o_ref[...] = dot_nn(nt_ref[...], p_ref[...]).astype(b16)


def entry_grad(normed_t, piece):
    rows, width = piece.shape
    return pl.pallas_call(
        entry_grad_body,
        grid=(width // CB,),
        in_specs=[whole_spec(normed_t.shape), pl.BlockSpec((rows, CB), lambda j: (0, j))],
        out_specs=pl.BlockSpec((D, CB), lambda j: (0, j)),
        out_shape=jax.ShapeDtypeStruct((D, width), b16),
        name="entry_grad",
    )(normed_t, piece)


def bit_orders(count):
    bits = list(range(count))
    return [bits[k % count :] + bits[: k % count] for k in range(3)]


def partners(size, bit):
    return [(i, i ^ (1 << bit)) for i in range(size)]


def gather_rows(shard, order, size, f_pos, s_pos):
    have = []
    value = shard
    for bit in reversed(order):
        got = lax.ppermute(value, "fsdp", partners(size, bit))
        mine = ((f_pos >> bit) & 1) == 0
        axis = sum(1 for other in have if other > bit)
        value = jnp.stack([jnp.where(mine, value, got), jnp.where(mine, got, value)], axis=axis)
        have.append(bit)
    got = lax.ppermute(value, "seq", SWAP)
    mine = s_pos == 0
    value = jnp.stack(
        [jnp.where(mine, value, got), jnp.where(mine, got, value)], axis=len(have)
    )
    return value.reshape(-1, shard.shape[-1])


def scatter_rows(grad, order, size, f_pos, s_pos):
    rows = grad.shape[0] // (2 * size)
    width = grad.shape[1]
    value = grad.reshape(size, 2, rows, width)
    keep = lax.dynamic_index_in_dim(value, s_pos, 1, keepdims=False)
    send = lax.dynamic_index_in_dim(value, 1 - s_pos, 1, keepdims=False)
    got = lax.ppermute(send, "seq", SWAP)
    value = (keep.astype(f32) + got.astype(f32)).astype(b16)
    have = sorted(order, reverse=True)
    value = value.reshape((2,) * len(have) + (rows, width))
    for step, bit in enumerate(order):
        axis = have.index(bit)
        mine = (f_pos >> bit) & 1
        keep = lax.dynamic_index_in_dim(value, mine, axis, keepdims=False)
        send = lax.dynamic_index_in_dim(value, 1 - mine, axis, keepdims=False)
        got = lax.ppermute(send, "fsdp", partners(size, bit))
        value = keep.astype(f32) + got.astype(f32)
        if step + 1 < len(order):
            value = value.astype(b16)
        have.pop(axis)
    return value


def butterfly(value, size):
    value = value + lax.ppermute(value, "seq", SWAP)
    bit = 0
    while (1 << bit) < size:
        value = value + lax.ppermute(value, "fsdp", partners(size, bit))
        bit += 1
    return value


def exchange(value):
    return lax.all_to_all(value, "seq", split_axis=0, concat_axis=0, tiled=True)


def adam_update(master, moment_one, second, gradient, factor):
    clipped = gradient * factor
    new_one = beta_first * moment_one + (1.0 - beta_first) * clipped
    new_second = beta_second * second + (1.0 - beta_second) * clipped * clipped
    one_hat = new_one / (1.0 - beta_first**STEP)
    second_hat = new_second / (1.0 - beta_second**STEP)
    new_master = master - learn_rate * (
        one_hat / (jnp.sqrt(second_hat) + adam_eps) + decay_rate * master
    )
    return (new_master, new_one, new_second)


def per_device(
    tokens,
    cotangent,
    lengths,
    master_in,
    master_qkv,
    master_ssm_out,
    master_att_out,
    master_gu,
    master_down,
    master_small,
    *state,
):
    moments = state[:7]
    squares = state[7:]
    f_size = lax.axis_size("fsdp")
    f_pos = lax.axis_index("fsdp")
    s_pos = lax.axis_index("seq")
    devices = 2 * f_size
    tok_rows = tokens.shape[0]
    length = 2 * tok_rows
    per_group = NHM // 2
    bits = f_size.bit_length() - 1
    orders = bit_orders(bits)

    def cut(array, first, width):
        return array[:, first : first + width].astype(b16)

    own_rows = master_in.shape[0]
    fill = jnp.zeros((own_rows, 128 - per_group), b16)
    shards = []
    for g in range(2):
        shards.append(
            jnp.concatenate(
                [
                    cut(master_in, DSSM + GX * g, GX),
                    cut(master_qkv, GQ * g, GQ),
                    cut(master_qkv, HQ * HD + HD * g, HD),
                    cut(master_qkv, (HQ + HK) * HD + HD * g, HD),
                    cut(master_in, 2 * DSSM + BCW + per_group * g, per_group),
                    fill,
                ],
                axis=1,
            )
        )
    shards.append(jnp.concatenate([cut(master_in, 2 * DSSM, BCW), cut(master_in, 0, DSSM)], axis=1))
    mid_rows = (
        master_ssm_out.shape[0], master_att_out.shape[0], master_down.shape[0],
        own_rows, own_rows, own_rows, own_rows,
    )
    mid_shard = jnp.concatenate(
        [master_ssm_out.astype(b16), master_att_out.astype(b16), master_down.astype(b16)]
        + [cut(master_gu, D * b, D) for b in range(4)],
        axis=0,
    )
    w_mid = lax.all_gather(mid_shard, BOTH, axis=0, tiled=True).reshape(devices, sum(mid_rows), D)
    w0, w1, w2 = [gather_rows(shards[i], orders[i], f_size, f_pos, s_pos) for i in range(3)]
    if devices != PSEUDO:
        pieces = []
        first = 0
        for rows in mid_rows:
            pieces.append(w_mid[:, first : first + rows].reshape(PSEUDO, -1, D))
            first = first + rows
        w_mid = jnp.concatenate(pieces, axis=1)

    gain_in, gain_ff, gain_ssm, conv_bias, conv_weight, dt_bias, a_log, d_skip = split_small(
        master_small
    )
    slot_positions = s_pos * tok_rows + jnp.arange(tok_rows, dtype=jnp.int32)
    keep = (slot_positions < lengths[0]).astype(f32)[:, None]
    x_value = tokens.astype(f32)
    normed = (x_value * rms_scale(x_value) * gain_in).astype(b16)
    normed_t = normed.T
    cos, sin = rope_rows(length)
    rot = turn_matrix()
    seg = (
        lax.broadcasted_iota(jnp.int32, (GX, 128), 0) // HDM
        == lax.broadcasted_iota(jnp.int32, (GX, 128), 1)
    ).astype(b16)
    x_offset = s_pos * GX
    head_offset = s_pos * per_group
    conv_cols = jnp.concatenate(
        [lax.dynamic_slice_in_dim(conv_weight, x_offset, GX, 1), conv_weight[:, DSSM:]], axis=1
    )
    conv_rows = jnp.concatenate([conv_cols, jnp.zeros((8 - KCONV, GX + BCW), f32)], axis=0)
    bias_row = jnp.concatenate(
        [lax.dynamic_slice_in_dim(conv_bias, x_offset, GX, 0), conv_bias[DSSM:]]
    )[None]
    heads = lambda v: lax.dynamic_slice_in_dim(v, head_offset, per_group, 0)
    wide = lambda v: jnp.pad(v, (0, 128 - per_group))
    head_rows = jnp.pad(
        jnp.stack([wide(heads(dt_bias)), wide(-jnp.exp(heads(a_log)))]), ((0, 6), (0, 0))
    )
    skip_row = jnp.repeat(heads(d_skip), HDM)[None]

    mixed = exchange(project_send(normed, w0, w1, w2)).reshape(length, GCOLS + BCW)
    z_gate = project_gate(normed, w2)
    att_out, lse = attn_fwd(mixed, cos, sin, rot, GQ)
    att_back = exchange(att_out.reshape(2, tok_rows, GQ))
    y_out, states = mamba_fwd(mixed, conv_rows, bias_row, head_rows, skip_row, GX)
    ys_back = exchange(y_out.reshape(2, tok_rows, GX))
    (
        output, d_residual, ssm_norm, ff_in, hidden, d_gate_up, d_branch, d_mixer, d_ys, d_att, d_z,
        grad_gain_ff, grad_gain_ssm,
    ) = middle(
        tokens, cotangent, keep, ys_back, att_back, z_gate, w_mid, gain_ff[None], gain_ssm[None]
    )
    mid_grads = middle_grads(ff_in, hidden, ssm_norm, att_back, d_gate_up, d_branch, d_mixer)
    if devices != PSEUDO:
        pieces = []
        first = 0
        for rows in mid_rows:
            rows = rows * devices // PSEUDO
            pieces.append(mid_grads[:, first : first + rows].reshape(devices, -1, D))
            first = first + rows
        mid_grads = jnp.concatenate(pieces, axis=1)
    mid_owned = lax.psum_scatter(
        mid_grads.reshape(-1, D), BOTH, scatter_dimension=0, tiled=True
    ).astype(f32)
    d_att_rows = exchange(d_att).reshape(length, GQ)
    d_y_rows = exchange(d_ys).reshape(length, GX)
    att_grads = attn_bwd(mixed, cos, sin, rot, lse, d_att_rows)
    att_grads = exchange(att_grads.reshape(2, tok_rows, -1))
    mix_grads, conv_grads, head_grads, skip_grads = mamba_bwd(
        mixed, d_y_rows, states, conv_rows, bias_row, head_rows, skip_row, seg, GX
    )
    mix_grads = exchange(mix_grads.reshape(2, tok_rows, -1))
    token_grad, p0, p1, p2, grad_gain_in = entry_back(
        tokens, d_residual, mix_grads, att_grads, d_z, w0, w1, w2, gain_in[None]
    )
    o0, o1, o2 = [
        scatter_rows(entry_grad(normed_t, piece), orders[i], f_size, f_pos, s_pos)
        for i, piece in enumerate((p0, p1, p2))
    ]
    grad_in = jnp.concatenate(
        [
            o2[:, BCW:], o0[:, :GX], o1[:, :GX], o2[:, :BCW],
            o0[:, GDT : GDT + per_group], o1[:, GDT : GDT + per_group],
        ],
        axis=1,
    )
    grad_qkv = jnp.concatenate(
        [
            o0[:, GX : GX + GQ], o1[:, GX : GX + GQ],
            o0[:, GX + GQ : GX + GQ + HD], o1[:, GX + GQ : GX + GQ + HD],
            o0[:, GX + GQ + HD : GDT], o1[:, GX + GQ + HD : GDT],
        ],
        axis=1,
    )
    mid_pieces = []
    first = 0
    for rows in mid_rows:
        mid_pieces.append(mid_owned[first : first + rows])
        first = first + rows
    grad_gu = jnp.concatenate(mid_pieces[3:], axis=1)
    owned = (grad_in, grad_qkv, mid_pieces[0], mid_pieces[1], grad_gu, mid_pieces[2])

    conv_bias_grad = jnp.concatenate(
        [
            lax.dynamic_update_slice_in_dim(
                jnp.zeros((DSSM,), f32), conv_grads[KCONV, :GX], x_offset, 0
            ),
            conv_grads[KCONV, GX:],
        ]
    )
    conv_weight_grad = jnp.concatenate(
        [
            lax.dynamic_update_slice_in_dim(
                jnp.zeros((KCONV, DSSM), f32), conv_grads[:KCONV, :GX], x_offset, 1
            ),
            conv_grads[:KCONV, GX:],
        ],
        axis=1,
    )
    head_zeros = jnp.zeros((NHM,), f32)
    place = lambda v: lax.dynamic_update_slice_in_dim(head_zeros, v, head_offset, 0)
    small_local = jnp.concatenate(
        [
            grad_gain_in[0],
            grad_gain_ff[0],
            grad_gain_ssm[0],
            conv_bias_grad,
            conv_weight_grad.reshape(KCONV * CONVW),
            place(head_grads[0, :per_group]),
            place(head_grads[1, :per_group]),
            place(jnp.sum(skip_grads[0].reshape(per_group, HDM), axis=1)),
        ]
    )
    n_small = small_local.shape[0]
    small_rows = jnp.pad(small_local, (0, -n_small % 1024)).reshape(-1, 128)
    small_total = butterfly(small_rows, f_size).reshape(-1)[:n_small]
    local_square = jnp.zeros((), f32)
    for g in owned:
        local_square = local_square + jnp.sum(g * g)
    square_total = butterfly(jnp.broadcast_to(local_square, (8, 128)), f_size)[0, 0] + jnp.sum(
        small_total * small_total
    )
    grad_norm = jnp.sqrt(square_total)
    factor = jnp.minimum(1.0, clip_norm / (grad_norm + 1e-06))
    all_grads = owned + (small_total,)
    masters = (
        master_in,
        master_qkv,
        master_ssm_out,
        master_att_out,
        master_gu,
        master_down,
        master_small,
    )
    updated = [
        adam_update(masters[i], moments[i], squares[i], all_grads[i], factor) for i in range(7)
    ]
    return (
        (output, token_grad, grad_norm)
        + all_grads
        + tuple(updated[i][0] for i in range(6))
        + (updated[6][0] - master_small,)
        + tuple(updated[i][1] for i in range(7))
        + tuple(updated[i][2] for i in range(7))
    )


def solution(mesh):
    rows = P(BOTH, None)
    weights = (rows,) * 6 + (P(),)
    return jax.shard_map(
        per_device,
        mesh=mesh,
        in_specs=(rows, rows, P("fsdp")) + weights * 3,
        out_specs=(rows, rows, P()) + weights * 4,
        check_vma=False,
    )
```

```python
import jax
import jax.numpy as jnp
from jax import lax
from jax.experimental import pallas as pl
from jax.experimental.pallas import tpu as pltpu

f32 = jnp.float32
b16 = jnp.bfloat16
BL = 128
HDM = 64
NSTATE = 128
HD = 64
KCONV = 4
NEG = -1e30


def dot_nn(a, b):
    return lax.dot_general(a, b, (((1,), (0,)), ((), ())), preferred_element_type=f32)


def dot_nt(a, b):
    return lax.dot_general(a, b, (((1,), (1,)), ((), ())), preferred_element_type=f32)


def dot_tn(a, b):
    return lax.dot_general(a, b, (((0,), (0,)), ((), ())), preferred_element_type=f32)


def dot_exact(a, b):
    return lax.dot_general(
        a, b, (((1,), (0,)), ((), ())), preferred_element_type=f32, precision=lax.Precision.HIGHEST
    )


def lane_iota(shape):
    return lax.broadcasted_iota(jnp.int32, shape, 1)


def spread_heads(cols, pairs):
    low_half = lane_iota((cols.shape[0], 128)) < HDM
    return jnp.concatenate(
        [
            jnp.where(low_half, cols[:, 2 * k : 2 * k + 1], cols[:, 2 * k + 1 : 2 * k + 2])
            for k in range(pairs)
        ],
        axis=1,
    )


def halves(pair):
    low_half = lane_iota(pair.shape) < HDM
    zero = jnp.zeros_like(pair)
    return jnp.where(low_half, pair, zero), jnp.where(low_half, zero, pair)


def conv_parts(x_ref, bc_ref, halo, cw_ref, cb_ref):
    u = jnp.concatenate([x_ref[...], bc_ref[...]], axis=1).astype(f32)
    ext = jnp.concatenate([halo, u], axis=0)
    pre = cb_ref[...] + jnp.zeros_like(u)
    for k in range(KCONV):
        pre = pre + cw_ref[k : k + 1, :] * ext[5 + k : 5 + k + BL]
    sig = 1.0 / (1.0 + jnp.exp(-pre))
    return u, ext, pre, sig


def step_parts(dt_ref, hp_ref):
    raw = dt_ref[...].astype(f32) + hp_ref[0:1, :]
    step = jnp.maximum(raw, 0.0) + jnp.log1p(jnp.exp(-jnp.abs(raw)))
    log_decay = hp_ref[1:2, :] * step
    row = lax.broadcasted_iota(jnp.int32, (BL, BL), 0)
    col = lax.broadcasted_iota(jnp.int32, (BL, BL), 1)
    tril = (row >= col).astype(f32)
    cum = dot_exact(tril, log_decay)
    return raw, step, log_decay, cum, row, col


def mamba_fwd_body(x_ref, bc_ref, dt_ref, cw_ref, cb_ref, hp_ref, dsk_ref, y_ref, hs_ref, state, halo):
    width = x_ref.shape[1]
    pairs = width // 128

    @pl.when(pl.program_id(0) == 0)
    def _():
        state[...] = jnp.zeros_like(state)
        halo[...] = jnp.zeros_like(halo)

    u, ext, pre, sig = conv_parts(x_ref, bc_ref, halo[...], cw_ref, cb_ref)
    halo[...] = u[BL - 8 :]
    act = pre * sig
    x = act[:, :width]
    b_low = act[:, width : width + NSTATE].astype(b16)
    c_low = act[:, width + NSTATE :].astype(b16)
    _, step, _, cum, row, col = step_parts(dt_ref, hp_ref)
    cum_t = cum.T
    keep = row >= col
    cb = dot_nt(c_low, b_low)
    ecum = spread_heads(jnp.exp(cum), pairs)
    to_end = spread_heads(jnp.exp(cum[BL - 1 : BL, :] - cum), pairs)
    xs = x * spread_heads(step, pairs)
    h_old = state[...]
    hs_ref[0] = h_old
    outer = dot_nn(c_low, h_old.astype(b16)) * ecum + dsk_ref[...] * x
    for k in range(pairs):
        mats = []
        for h in (2 * k, 2 * k + 1):
            diff = cum[:, h : h + 1] - cum_t[h : h + 1, :]
            mats.append((jnp.exp(jnp.where(keep, diff, NEG)) * cb).astype(b16))
        lo, hi = halves(xs[:, 128 * k : 128 * k + 128].astype(b16))
        inner = dot_nn(jnp.concatenate(mats, axis=1), jnp.concatenate([lo, hi], axis=0))
        y_ref[:, 128 * k : 128 * k + 128] = (
            inner + outer[:, 128 * k : 128 * k + 128]
        ).astype(y_ref.dtype)
    state[...] = h_old * ecum[BL - 1 : BL, :] + dot_tn(b_low, (xs * to_end).astype(b16))


def seg_sum(values, seg_ref):
    hi = values.astype(b16)
    lo = (values - hi.astype(f32)).astype(b16)
    return dot_nn(hi, seg_ref[...]) + dot_nn(lo, seg_ref[...])


def mamba_bwd_body(
    x_ref, bc_ref, dt_ref, xp_ref, bcp_ref, dy_ref, hs_ref, cw_ref, cb_ref, hp_ref, dsk_ref, seg_ref, after_ref,
    dmix_ref, dcw_ref, dhp_ref, dsk_grad_ref,
    dstate, halo_next, wrow, wcol,
):
    width = x_ref.shape[1]
    pairs = width // 128
    idx = pl.program_id(0)
    count = pl.num_programs(0)

    @pl.when(idx == 0)
    def _():
        dstate[...] = jnp.zeros_like(dstate)
        halo_next[...] = jnp.zeros_like(halo_next)
        wrow[...] = jnp.zeros_like(wrow)
        wcol[...] = jnp.zeros_like(wcol)
        dcw_ref[...] = jnp.zeros_like(dcw_ref)
        dhp_ref[...] = jnp.zeros_like(dhp_ref)
        dsk_grad_ref[...] = jnp.zeros_like(dsk_grad_ref)

    prev = jnp.concatenate([xp_ref[...], bcp_ref[...]], axis=1).astype(f32)[8:]
    prev = jnp.where(idx == count - 1, 0.0, prev)
    u, ext, pre, sig = conv_parts(x_ref, bc_ref, prev, cw_ref, cb_ref)
    act = pre * sig
    x = act[:, :width]
    b_low = act[:, width : width + NSTATE].astype(b16)
    c_low = act[:, width + NSTATE :].astype(b16)
    raw, step, log_decay, cum, row, col = step_parts(dt_ref, hp_ref)
    cum_t = cum.T
    keep_t = row <= col
    gt = dot_nt(b_low, c_low)
    ecum = spread_heads(jnp.exp(cum), pairs)
    to_end = spread_heads(jnp.exp(cum[BL - 1 : BL, :] - cum), pairs)
    step_wide = spread_heads(step, pairs)
    xs = x * step_wide
    xs_low = xs.astype(b16)
    dy_low = dy_ref[...]
    dy = dy_low.astype(f32)
    h_old = hs_ref[0]
    h_low = h_old.astype(b16)
    dh = dstate[...]
    dh_low = dh.astype(b16)
    ch = dot_nn(c_low, h_low)
    bds = dot_nn(b_low, dh_low)
    edy = ecum * dy
    edy_low = edy.astype(b16)
    z = xs * to_end
    d_c = dot_nt(edy_low, h_low)
    d_b = dot_nt(z.astype(b16), dh_low)
    q2 = z * bds
    q1 = edy * ch
    d_gt = jnp.zeros((BL, BL), f32)
    inners = []
    for k in range(pairs):
        dy_halves = halves(dy_low[:, 128 * k : 128 * k + 128])
        xs_pair = xs_low[:, 128 * k : 128 * k + 128]
        mats = []
        for j, h in enumerate((2 * k, 2 * k + 1)):
            diff = cum_t[h : h + 1, :] - cum[:, h : h + 1]
            lt = jnp.exp(jnp.where(keep_t, diff, NEG))
            d_mt = dot_nt(xs_pair, dy_halves[j]) * lt
            d_gt = d_gt + d_mt
            wt = d_mt * gt
            wrow[h : h + 1, :] = jnp.sum(wt, axis=0, keepdims=True)
            wcol[:, h : h + 1] = jnp.sum(wt, axis=1, keepdims=True)
            mats.append((lt * gt).astype(b16))
        inners.append(
            dot_nn(jnp.concatenate(mats, axis=1), jnp.concatenate(list(dy_halves), axis=0))
        )
    d_gt_low = d_gt.astype(b16)
    d_b = d_b + dot_nn(d_gt_low, c_low)
    d_c = d_c + dot_tn(d_gt_low, b_low)
    dxs = jnp.concatenate(inners, axis=1) + to_end * bds
    tail = jnp.sum(q2, axis=0, keepdims=True) + ecum[BL - 1 : BL, :] * jnp.sum(
        dh * h_old, axis=0, keepdims=True
    )
    tail_heads = seg_sum(jnp.broadcast_to(tail, (8, width)), seg_ref)[0:1, :]
    d_cum = seg_sum(q1 - q2, seg_ref) + wrow[...].T - wcol[...]
    d_cum = d_cum + jnp.where(row == BL - 1, tail_heads, 0.0)
    d_ld = dot_exact((row <= col).astype(f32), d_cum)
    d_step = seg_sum(dxs * x, seg_ref) + hp_ref[1:2, :] * d_ld
    d_raw = d_step / (1.0 + jnp.exp(-raw))
    dmix_ref[:, width : width + 128] = d_raw.astype(b16)
    dhp_ref[0:1, :] += jnp.sum(d_raw, axis=0, keepdims=True)
    dhp_ref[1:2, :] += jnp.sum(d_ld * log_decay, axis=0, keepdims=True)
    dsk_grad_ref[0:1, :] += jnp.sum(dy * x, axis=0, keepdims=True)
    dstate[...] = dh * ecum[BL - 1 : BL, :] + dot_tn(c_low, edy_low)
    d_x = dxs * step_wide + dsk_ref[...] * dy
    d_act = jnp.concatenate([d_x, d_b, d_c], axis=1)
    d_pre = d_act * sig * (1.0 + pre * (1.0 - sig))
    for k in range(KCONV):
        dcw_ref[k : k + 1, :] += jnp.sum(d_pre * ext[5 + k : 5 + k + BL], axis=0, keepdims=True)
    dcw_ref[KCONV : KCONV + 1, :] += jnp.sum(d_pre, axis=0, keepdims=True)
    ext_next = jnp.concatenate([d_pre, halo_next[...]], axis=0)
    halo_next[...] = d_pre[:8]
    du = jnp.zeros_like(d_pre)
    for k in range(KCONV):
        du = du + cw_ref[k : k + 1, :] * ext_next[3 - k : 3 - k + BL]
    dmix_ref[:, :width] = du[:, :width].astype(b16)
    dmix_ref[:, width + 128 :] = du[:, width:].astype(b16)


def mamba_fwd(mixed, conv_w, conv_b, head_rows, skip_row, width):
    length = mixed.shape[0]
    blocks = length // BL
    full = lambda shape: pl.BlockSpec(shape, lambda i: (0,) * len(shape))
    return pl.pallas_call(
        mamba_fwd_body,
        grid=(blocks,),
        in_specs=[
            pl.BlockSpec((BL, width), lambda i: (i, 0)),
            pl.BlockSpec((BL, 2 * NSTATE), lambda i: (i, 5)),
            pl.BlockSpec((BL, 128), lambda i: (i, 9)),
            full(conv_w.shape),
            full(conv_b.shape),
            full(head_rows.shape),
            full(skip_row.shape),
        ],
        out_specs=[
            pl.BlockSpec((BL, width), lambda i: (i, 0)),
            pl.BlockSpec((1, NSTATE, width), lambda i: (i, 0, 0)),
        ],
        out_shape=[
            jax.ShapeDtypeStruct((length, width), b16),
            jax.ShapeDtypeStruct((blocks, NSTATE, width), f32),
        ],
        scratch_shapes=[pltpu.VMEM((NSTATE, width), f32), pltpu.VMEM((8, width + 2 * NSTATE), f32)],
        compiler_params=pltpu.CompilerParams(dimension_semantics=("arbitrary",)),
        name="mamba_fwd",
    )(mixed, mixed, mixed, conv_w, conv_b, head_rows, skip_row)


def mamba_bwd(mixed, d_y, states, conv_w, conv_b, head_rows, skip_row, seg, after, width):
    length = mixed.shape[0]
    blocks = length // BL
    full = lambda shape: pl.BlockSpec(shape, lambda i: (0,) * len(shape))
    last = blocks - 1
    per = BL // 16
    back = lambda j: (lambda i: (last - i, j))
    prior = lambda j: (lambda i: (jnp.maximum((last - i) * per - 1, 0), j))
    return pl.pallas_call(
        mamba_bwd_body,
        grid=(blocks,),
        in_specs=[
            pl.BlockSpec((BL, width), back(0)),
            pl.BlockSpec((BL, 2 * NSTATE), back(5)),
            pl.BlockSpec((BL, 128), back(9)),
            pl.BlockSpec((16, width), prior(0)),
            pl.BlockSpec((16, 2 * NSTATE), prior(5)),
            pl.BlockSpec((BL, width), back(0)),
            pl.BlockSpec((1, NSTATE, width), lambda i: (last - i, 0, 0)),
            full(conv_w.shape),
            full(conv_b.shape),
            full(head_rows.shape),
            full(skip_row.shape),
            full(seg.shape),
            pl.BlockSpec((16, 128), lambda i: (0, 0)),
        ],
        out_specs=[
            pl.BlockSpec((BL, width + 128 + 2 * NSTATE), back(0)),
            full((8, width + 2 * NSTATE)),
            full((8, 128)),
            full((8, width)),
        ],
        out_shape=[
            jax.ShapeDtypeStruct((length, width + 128 + 2 * NSTATE), b16),
            jax.ShapeDtypeStruct((8, width + 2 * NSTATE), f32),
            jax.ShapeDtypeStruct((8, 128), f32),
            jax.ShapeDtypeStruct((8, width), f32),
        ],
        scratch_shapes=[
            pltpu.VMEM((NSTATE, width), f32),
            pltpu.VMEM((8, width + 2 * NSTATE), f32),
            pltpu.VMEM((BL, 128), f32),
            pltpu.VMEM((BL, 128), f32),
        ],
        compiler_params=pltpu.CompilerParams(dimension_semantics=("arbitrary",)),
        name="mamba_bwd",
    )(mixed, mixed, mixed, mixed, mixed, d_y, states, conv_w, conv_b, head_rows, skip_row, seg, after)


QB = 512


def turn(values, rot):
    return dot_nn(values, rot)


def rotated(att_ref, cos_ref, sin_ref, rot_ref, q_s, kk_s, vv_s, nq):
    cos = cos_ref[...]
    sin = sin_ref[...]
    rot = rot_ref[...]
    for p in range(nq):
        raw = att_ref[:, 128 * p : 128 * p + 128]
        q_s[:, 128 * p : 128 * p + 128] = (raw.astype(f32) * cos + turn(raw, rot) * sin).astype(b16)
    kv = att_ref[:, 128 * nq : 128 * nq + 128]
    low_half = lane_iota(kv.shape) < HD
    kv_wide = kv.astype(f32)
    kv_swap = pltpu.roll(kv_wide, HD, 1)
    kk = jnp.where(low_half, kv_wide, kv_swap).astype(b16)
    vv_s[...] = jnp.where(low_half, kv_swap, kv_wide).astype(b16)
    kk_s[...] = (kk.astype(f32) * cos + turn(kk, rot) * sin).astype(b16)


def attn_fwd_body(att_ref, cos_ref, sin_ref, rot_ref, o_ref, lse_ref, q_s, kk_s, vv_s):
    length = att_ref.shape[0]
    nq = o_ref.shape[1] // 128
    rotated(att_ref, cos_ref, sin_ref, rot_ref, q_s, kk_s, vv_s, nq)
    scale = HD ** (-0.5)
    for qi in range(length // QB):
        n = (qi + 1) * QB
        row = lax.broadcasted_iota(jnp.int32, (QB, QB), 0)
        col = lax.broadcasted_iota(jnp.int32, (QB, QB), 1)
        for p in range(nq):
            q_halves = halves(q_s[qi * QB : n, 128 * p : 128 * p + 128])
            v_halves = halves(vv_s[0:n, :])
            out = jnp.zeros((QB, 128), f32)
            for j in range(2):
                s = dot_nt(q_halves[j], kk_s[0:n, :]) * scale
                diag = jnp.where(row >= col, s[:, n - QB :], NEG)
                s = diag if qi == 0 else jnp.concatenate([s[:, : n - QB], diag], axis=1)
                top = jnp.max(s, axis=1, keepdims=True)
                e = jnp.exp(s - top)
                total = jnp.sum(e, axis=1, keepdims=True)
                w = (e * (1.0 / total)).astype(b16)
                out = out + dot_nn(w, v_halves[j])
                h = 2 * p + j
                lse_ref[qi * QB : n, h : h + 1] = top + jnp.log(total)
            o_ref[qi * QB : n, 128 * p : 128 * p + 128] = out.astype(o_ref.dtype)


def attn_bwd_body(
    att_ref, cos_ref, sin_ref, rot_ref, rot_t_ref, lse_ref, do_ref, d_ref, q_s, kk_s, vv_s, dk_s, dv_s
):
    length = att_ref.shape[0]
    nq = do_ref.shape[1] // 128
    rotated(att_ref, cos_ref, sin_ref, rot_ref, q_s, kk_s, vv_s, nq)
    scale = HD ** (-0.5)
    dk_s[...] = jnp.zeros_like(dk_s)
    dv_s[...] = jnp.zeros_like(dv_s)
    rot_t = rot_t_ref[...]
    kk_t = kk_s[...].astype(f32).T
    sub_low = lax.broadcasted_iota(jnp.int32, kk_t.shape, 0) < HD
    kt_halves = (
        jnp.where(sub_low, kk_t, 0.0).astype(b16),
        jnp.where(sub_low, 0.0, kk_t).astype(b16),
    )
    row = lax.broadcasted_iota(jnp.int32, (QB, QB), 0)
    col = lax.broadcasted_iota(jnp.int32, (QB, QB), 1)
    for qi in range(length // QB):
        rows = slice(qi * QB, (qi + 1) * QB)
        lse_t = lse_ref[rows, :].T
        for p in range(nq):
            q_halves = halves(q_s[rows, 128 * p : 128 * p + 128])
            do_halves = halves(do_ref[rows, 128 * p : 128 * p + 128])
            dq_t = jnp.zeros((128, QB), f32)
            for j in range(2):
                h = 2 * p + j
                weights = []
                d_weights = []
                dots = jnp.zeros((1, QB), f32)
                for kj in range(qi + 1):
                    keys = slice(kj * QB, (kj + 1) * QB)
                    s = dot_nt(kk_s[keys, :], q_halves[j]) * scale - lse_t[h : h + 1, :]
                    if kj == qi:
                        s = jnp.where(row <= col, s, NEG)
                    w = jnp.exp(s)
                    dw = dot_nt(vv_s[keys, :], do_halves[j])
                    dots = dots + jnp.sum(w * dw, axis=0, keepdims=True)
                    weights.append(w)
                    d_weights.append(dw)
                for kj in range(qi + 1):
                    keys = slice(kj * QB, (kj + 1) * QB)
                    ds = (weights[kj] * (d_weights[kj] - dots)).astype(b16)
                    dv_s[keys, :] += dot_nn(weights[kj].astype(b16), do_halves[j])
                    dk_s[keys, :] += dot_nn(ds, q_halves[j])
                    dq_t = dq_t + dot_nn(kt_halves[j][:, keys], ds)
            dq = dq_t.T * scale
            cos = cos_ref[rows, :]
            sin = sin_ref[rows, :]
            back = dq * cos + dot_exact(dq * sin, rot_t)
            d_ref[rows, 128 * p : 128 * p + 128] = back.astype(b16)
    low_half = lane_iota(dk_s.shape) < HD
    dk = dk_s[...] * scale
    dk = dk + pltpu.roll(dk, HD, 1)
    dv = dv_s[...]
    dv = dv + pltpu.roll(dv, HD, 1)
    dk = dk * cos_ref[...] + dot_exact(dk * sin_ref[...], rot_t)
    d_ref[:, 128 * nq : 128 * nq + 128] = jnp.where(low_half, dk, dv).astype(b16)


def rope_rows(length):
    half_dim = HD // 2
    positions = jnp.arange(length, dtype=f32)
    frequency = 10000.0 ** (-jnp.arange(half_dim, dtype=f32) * 2.0 / HD)
    angles = positions[:, None] * frequency[None, :]
    cosine = jnp.cos(angles)
    sine = jnp.sin(angles)
    return jnp.concatenate([cosine] * 4, axis=1), jnp.concatenate([sine] * 4, axis=1)


def turn_matrix():
    row = lax.broadcasted_iota(jnp.int32, (128, 128), 0)
    col = lax.broadcasted_iota(jnp.int32, (128, 128), 1)
    same = (row // HD) == (col // HD)
    plus = same & (col - row == HD // 2)
    minus = same & (row - col == HD // 2)
    return plus.astype(f32) - minus.astype(f32)


def attn_fwd(mixed, cos, sin, rot, q_width):
    length = mixed.shape[0]
    width = q_width + 128
    spec = lambda shape: pl.BlockSpec(shape, lambda i: (0,) * len(shape))
    return pl.pallas_call(
        attn_fwd_body,
        grid=(1,),
        in_specs=[
            pl.BlockSpec((length, width), lambda i: (0, 2)),
            spec((length, 128)),
            spec((length, 128)),
            spec((128, 128)),
        ],
        out_specs=[spec((length, q_width)), spec((length, 128))],
        out_shape=[
            jax.ShapeDtypeStruct((length, q_width), b16),
            jax.ShapeDtypeStruct((length, 128), f32),
        ],
        scratch_shapes=[
            pltpu.VMEM((length, q_width), b16),
            pltpu.VMEM((length, 128), b16),
            pltpu.VMEM((length, 128), b16),
        ],
        name="attn_fwd",
    )(mixed, cos, sin, rot.astype(b16))


def attn_bwd(mixed, cos, sin, rot, lse, d_out):
    length = mixed.shape[0]
    q_width = d_out.shape[1]
    width = q_width + 128
    spec = lambda shape: pl.BlockSpec(shape, lambda i: (0,) * len(shape))
    return pl.pallas_call(
        attn_bwd_body,
        grid=(1,),
        in_specs=[
            pl.BlockSpec((length, width), lambda i: (0, 2)),
            spec((length, 128)),
            spec((length, 128)),
            spec((128, 128)),
            spec((128, 128)),
            spec((length, 128)),
            spec((length, q_width)),
        ],
        out_specs=spec((length, width)),
        out_shape=jax.ShapeDtypeStruct((length, width), b16),
        scratch_shapes=[
            pltpu.VMEM((length, q_width), b16),
            pltpu.VMEM((length, 128), b16),
            pltpu.VMEM((length, 128), b16),
            pltpu.VMEM((length, 128), f32),
            pltpu.VMEM((length, 128), f32),
        ],
        name="attn_bwd",
    )(mixed, cos, sin, rot.astype(b16), rot.T, lse, d_out)


from jax.sharding import PartitionSpec as P

D = 1024
FF = 2048
NHM = 24
HQ = 8
HK = 2
STEP = 10
DSSM = 1536
CONVW = 1792
GX = DSSM // 2
GQ = HQ // 2 * HD
GCOLS = GX + GQ + 2 * HD + 128
GDT = GX + GQ + 2 * HD
BCW = 2 * NSTATE
RB = 256
CB = 256
PSEUDO = 32

norm_eps = 1e-05
beta_first = 0.9
beta_second = 0.999
adam_eps = 1e-08
learn_rate = 0.04
decay_rate = 0.1
clip_norm = 1.0
BOTH = ("fsdp", "seq")
SWAP = [(0, 1), (1, 0)]


def whole_spec(shape):
    return pl.BlockSpec(shape, lambda *_: (0,) * len(shape))


def held_spec(shape):
    return pl.BlockSpec(shape, lambda *_: (0,) * len(shape), pipeline_mode=pl.Buffered(1))


def split_small(vector):
    widths = [D, D, DSSM, CONVW, KCONV * CONVW, NHM, NHM, NHM]
    pieces = []
    offset = 0
    for piece_width in widths:
        pieces.append(vector[offset : offset + piece_width])
        offset = offset + piece_width
    gain_in, gain_ff, gain_ssm, conv_bias, conv_flat, dt_bias, a_log, d_skip = pieces
    return (
        gain_in,
        gain_ff,
        gain_ssm,
        conv_bias,
        conv_flat.reshape(KCONV, CONVW),
        dt_bias,
        a_log,
        d_skip,
    )


def send_body(n_ref, w0_ref, w1_ref, w2_ref, o_ref):
    g = pl.program_id(0)
    j = pl.program_id(1)
    last = pl.num_programs(1) - 1

    @pl.when((j < last) & (g == 0))
    def _():
        o_ref[0] = dot_nn(n_ref[...], w0_ref[...]).astype(b16)

    @pl.when((j < last) & (g == 1))
    def _():
        o_ref[0] = dot_nn(n_ref[...], w1_ref[...]).astype(b16)

    @pl.when(j == last)
    def _():
        o_ref[0] = dot_nn(n_ref[...], w2_ref[...]).astype(b16)


def project_send(normed, w0, w1, w2):
    rows = normed.shape[0]
    nb = GCOLS // CB
    return pl.pallas_call(
        send_body,
        grid=(2, nb + 1),
        in_specs=[
            whole_spec(normed.shape),
            pl.BlockSpec((D, CB), lambda g, j: (0, jnp.where(g == 0, jnp.minimum(j, nb - 1), nb - 1))),
            pl.BlockSpec((D, CB), lambda g, j: (0, jnp.where(g == 1, jnp.minimum(j, nb - 1), 0))),
            pl.BlockSpec((D, CB), lambda g, j: (0, 0)),
        ],
        out_specs=pl.BlockSpec((1, rows, CB), lambda g, j: (g, 0, j)),
        out_shape=jax.ShapeDtypeStruct((2, rows, GCOLS + BCW), b16),
        name="project_send",
    )(normed, w0, w1, w2)


def gate_body(n_ref, wide_ref, left_ref, right_ref, o_ref):
    j = pl.program_id(0)

    @pl.when(j < D // CB)
    def _():
        o_ref[...] = dot_nn(n_ref[...], wide_ref[...].reshape(D, CB))

    @pl.when(j >= D // CB)
    def _():
        o_ref[...] = dot_nn(n_ref[...], join_rows(left_ref[...], right_ref[...]))


def join_rows(left, right):
    return jnp.concatenate([left, right], axis=1).reshape(D, left.shape[2])


def project_gate(normed, weights):
    rows = normed.shape[0]
    nb = D // CB
    half = nb // 2
    return pl.pallas_call(
        gate_body,
        grid=(DSSM // CB,),
        in_specs=[
            whole_spec(normed.shape),
            pl.BlockSpec((PSEUDO, 32, CB), lambda j: (0, 8, jnp.minimum(j, nb - 1))),
            pl.BlockSpec((PSEUDO, 16, CB), lambda j: (0, 18, jnp.maximum(j - nb, 0))),
            pl.BlockSpec((PSEUDO, 16, CB), lambda j: (0, 18, jnp.maximum(j - nb, 0) + half)),
        ],
        out_specs=pl.BlockSpec((rows, CB), lambda j: (0, j)),
        out_shape=jax.ShapeDtypeStruct((rows, DSSM), f32),
        name="project_gate",
    )(normed, weights, weights, weights)


def norm_back(values, scaling, gain_vec, d_normed):
    weighted = d_normed * gain_vec
    gain_grad = jnp.sum(d_normed * values * scaling, axis=0, keepdims=True)
    d_values = scaling * weighted - values * scaling**3 * jnp.mean(
        weighted * values, axis=-1, keepdims=True
    )
    return gain_grad, d_values


def rms_scale(values):
    return lax.rsqrt(jnp.mean(values * values, axis=-1, keepdims=True) + norm_eps)


def middle_body(
    tok_ref, cot_ref, keep_ref, ys_ref, att_ref, z_ref, w_ref, gff_ref, gssm_ref,
    out_ref, dres_ref, norm_ref, ffin_ref, hid_ref, dgu_ref, dbr_ref, dmix_ref, dys_ref, datt_ref, dz_ref,
    ggff_ref, ggssm_ref,
    gate_s, up_s,
):
    @pl.when(pl.program_id(0) == 0)
    def _():
        ggff_ref[...] = jnp.zeros_like(ggff_ref)
        ggssm_ref[...] = jnp.zeros_like(ggssm_ref)

    def weight(first, rows, lo=0, hi=PSEUDO):
        return w_ref[lo:hi, first : first + rows, :].reshape((hi - lo) * rows, D)

    w_so = lambda: weight(0, 48)
    w_ao = lambda: weight(48, 16)
    w_down = lambda b: weight(64, 64, 16 * b, 16 * b + 16)
    w_gu = lambda b: weight(128 + 32 * b, 32)

    ys = jnp.concatenate([ys_ref[0], ys_ref[1]], axis=1).astype(f32)
    z = z_ref[...]
    sig_z = 1.0 / (1.0 + jnp.exp(-z))
    silu_z = z * sig_z
    gated = ys * silu_z
    scale_ssm = rms_scale(gated)
    gain_ssm = gssm_ref[...]
    ssm_norm = (gated * scale_ssm * gain_ssm).astype(b16)
    norm_ref[...] = ssm_norm
    att = jnp.concatenate([att_ref[0], att_ref[1]], axis=1)
    residual = tok_ref[...].astype(f32) + (dot_nn(ssm_norm, w_so()) + dot_nn(att, w_ao()))
    scale_ff = rms_scale(residual)
    gain_ff = gff_ref[...]
    ff_in = (residual * scale_ff * gain_ff).astype(b16)
    ffin_ref[...] = ff_in
    branch = jnp.zeros_like(residual)
    for b in range(2):
        gate = dot_nn(ff_in, w_gu(b))
        up = dot_nn(ff_in, w_gu(b + 2))
        gate_s[b] = gate
        up_s[b] = up
        hidden = (gate * (1.0 / (1.0 + jnp.exp(-gate))) * up).astype(b16)
        hid_ref[:, D * b : D * b + D] = hidden
        branch = branch + dot_nn(hidden, w_down(b))
    keep = keep_ref[...]
    out_ref[...] = ((residual + branch) * keep).astype(b16)
    d_out = cot_ref[...].astype(f32) * keep
    d_branch = d_out.astype(b16)
    dbr_ref[...] = d_branch
    d_ff_in = jnp.zeros_like(residual)
    for b in range(2):
        gate = gate_s[b]
        up = up_s[b]
        sig = 1.0 / (1.0 + jnp.exp(-gate))
        d_hidden = dot_nt(d_branch, w_down(b))
        d_gate = (d_hidden * up * sig * (1.0 + gate * (1.0 - sig))).astype(b16)
        d_up = (d_hidden * gate * sig).astype(b16)
        dgu_ref[:, D * b : D * b + D] = d_gate
        dgu_ref[:, FF + D * b : FF + D * b + D] = d_up
        d_ff_in = d_ff_in + dot_nt(d_gate, w_gu(b)) + dot_nt(d_up, w_gu(b + 2))
    gain_grad, d_norm = norm_back(residual, scale_ff, gain_ff, d_ff_in)
    ggff_ref[0:1, :] += gain_grad
    d_residual = d_out + d_norm
    dres_ref[...] = d_residual
    d_mixer = d_residual.astype(b16)
    dmix_ref[...] = d_mixer
    d_att = dot_nt(d_mixer, w_ao()).astype(b16)
    datt_ref[0] = d_att[:, :GQ]
    datt_ref[1] = d_att[:, GQ:]
    gain_grad, d_gated = norm_back(gated, scale_ssm, gain_ssm, dot_nt(d_mixer, w_so()))
    ggssm_ref[0:1, :] += gain_grad
    d_ys = (d_gated * silu_z).astype(b16)
    dys_ref[0] = d_ys[:, :GX]
    dys_ref[1] = d_ys[:, GX:]
    dz_ref[...] = (d_gated * ys * sig_z * (1.0 + z * (1.0 - sig_z))).astype(b16)


def middle(tokens, cotangent, keep, ys, att, z, weights, gain_ff, gain_ssm):
    rows = tokens.shape[0]
    row = lambda width: pl.BlockSpec((RB, width), lambda i: (i, 0))
    pair = lambda width: pl.BlockSpec((2, RB, width), lambda i: (0, i, 0))
    sds = jax.ShapeDtypeStruct
    return pl.pallas_call(
        middle_body,
        grid=(rows // RB,),
        in_specs=[
            row(D), row(D), row(1), pair(GX), pair(GQ), row(DSSM),
            held_spec((PSEUDO, 256, D)), whole_spec((1, D)), whole_spec((1, DSSM)),
        ],
        out_specs=[
            row(D), row(D), row(DSSM), row(D), row(FF), row(2 * FF), row(D), row(D),
            pair(GX), pair(GQ), row(DSSM), whole_spec((8, D)), whole_spec((8, DSSM)),
        ],
        out_shape=[
            sds((rows, D), b16), sds((rows, D), f32), sds((rows, DSSM), b16), sds((rows, D), b16),
            sds((rows, FF), b16), sds((rows, 2 * FF), b16), sds((rows, D), b16), sds((rows, D), b16),
            sds((2, rows, GX), b16), sds((2, rows, GQ), b16), sds((rows, DSSM), b16),
            sds((8, D), f32), sds((8, DSSM), f32),
        ],
        scratch_shapes=[pltpu.VMEM((2, RB, D), f32), pltpu.VMEM((2, RB, D), f32)],
        compiler_params=pltpu.CompilerParams(vmem_limit_bytes=60 * 1024 * 1024),
        name="middle",
    )(tokens, cotangent, keep, ys, att, z, weights, gain_ff, gain_ssm)


def flip(values):
    return values.astype(f32).T.astype(b16)


def grads_body(
    ffin_ref, hid_ref, norm_ref, att_ref, g0_ref, g1_ref, g2_ref, g3_ref, dbr_ref, dmix_ref,
    o_ref, ffin_t, hid_t, norm_t, att_t,
):
    @pl.when(pl.program_id(0) == 0)
    def _():
        ffin_t[...] = flip(ffin_ref[...])
        hid_t[...] = flip(hid_ref[...])
        norm_t[...] = flip(norm_ref[...])
        att_t[:GQ, :] = flip(att_ref[0])
        att_t[GQ:, :] = flip(att_ref[1])

    def put(first, rows, value):
        o_ref[:, first : first + rows, :] = value.astype(b16).reshape(PSEUDO, rows, CB)

    put(0, 48, dot_nn(norm_t[...], dmix_ref[...]))
    put(48, 16, dot_nn(att_t[...], dmix_ref[...]))
    put(64, 64, dot_nn(hid_t[...], dbr_ref[...]))
    for b, g_ref in enumerate((g0_ref, g1_ref, g2_ref, g3_ref)):
        put(128 + 32 * b, 32, dot_nn(ffin_t[...], g_ref[...]))


def middle_grads(ff_in, hidden, ssm_norm, att, d_gate_up, d_branch, d_mixer):
    rows = ff_in.shape[0]
    nb = D // CB
    col = lambda first: pl.BlockSpec((rows, CB), lambda j: (0, first + j))
    return pl.pallas_call(
        grads_body,
        grid=(nb,),
        in_specs=[
            held_spec(ff_in.shape), held_spec(hidden.shape), held_spec(ssm_norm.shape), held_spec(att.shape),
            col(0), col(nb), col(2 * nb), col(3 * nb), col(0), col(0),
        ],
        out_specs=pl.BlockSpec((PSEUDO, 256, CB), lambda j: (0, 0, j)),
        out_shape=jax.ShapeDtypeStruct((PSEUDO, 256, D), b16),
        scratch_shapes=[
            pltpu.VMEM((D, rows), b16), pltpu.VMEM((FF, rows), b16),
            pltpu.VMEM((DSSM, rows), b16), pltpu.VMEM((2 * GQ, rows), b16),
        ],
        compiler_params=pltpu.CompilerParams(vmem_limit_bytes=60 * 1024 * 1024),
        name="middle_grads",
    )(ff_in, hidden, ssm_norm, att, d_gate_up, d_gate_up, d_gate_up, d_gate_up, d_branch, d_mixer)


def entry_body(tok_ref, dres_ref, dm_ref, da_ref, dz_ref, w0_ref, w1_ref, w2_ref, wz_ref, wf_ref, gin_ref,
               *rest):
    tg_ref, gg_ref = rest[-2:]

    @pl.when(pl.program_id(0) == 0)
    def _():
        gg_ref[...] = jnp.zeros_like(gg_ref)

    d_normed = jnp.zeros(tok_ref.shape, f32)
    for g, w_ref in enumerate((w0_ref, w1_ref)):
        piece = jnp.concatenate(
            [dm_ref[g][:, :GX], da_ref[g], dm_ref[g][:, GX : GX + 128]], axis=1
        )
        d_normed = d_normed + dot_nt(piece, w_ref[...])
    d_normed = d_normed + dot_nt(low_sum(dm_ref), w2_ref[...])
    d_normed = d_normed + dot_nt(dz_ref[:, :D], wz_ref[...].reshape(D, D))
    half = D // 2
    d_normed = d_normed + dot_nt(
        dz_ref[:, D:], join_rows(wf_ref[:, :, :half], wf_ref[:, :, half:])
    )
    x = tok_ref[...].astype(f32)
    gain_grad, d_x = norm_back(x, rms_scale(x), gin_ref[...], d_normed)
    gg_ref[0:1, :] += gain_grad
    tg_ref[...] = dres_ref[...] + d_x


def low_sum(dm_ref):
    return (
        dm_ref[0][:, GX + 128 :].astype(f32) + dm_ref[1][:, GX + 128 :].astype(f32)
    ).astype(b16)


def entry_back(tokens, d_residual, d_mix, d_att, d_z, w0, w1, w2, weights, gain_in, after):
    rows = tokens.shape[0]
    row = lambda width: pl.BlockSpec((RB, width), lambda i: (i, 0))
    pair = lambda width: pl.BlockSpec((2, RB, width), lambda i: (0, i, 0))
    once = pl.Buffered(1)
    sds = jax.ShapeDtypeStruct
    return pl.pallas_call(
        entry_body,
        grid=(rows // RB,),
        in_specs=[
            row(D), row(D), pair(d_mix.shape[2]), pair(d_att.shape[2]), row(DSSM),
            held_spec(w0.shape), held_spec(w1.shape), held_spec(w2.shape),
            pl.BlockSpec((PSEUDO, 32, D), lambda i: (0, 8, 0), pipeline_mode=once),
            pl.BlockSpec((PSEUDO, 16, D), lambda i: (0, 18, 0), pipeline_mode=once),
            whole_spec((1, D)),
        ]
        + [pl.BlockSpec((16, 128), lambda i: (0, 0))] * len(after),
        out_specs=[row(D), whole_spec((8, D))],
        out_shape=[sds((rows, D), f32), sds((8, D), f32)],
        compiler_params=pltpu.CompilerParams(vmem_limit_bytes=60 * 1024 * 1024),
        name="entry_back",
    )(tokens, d_residual, d_mix, d_att, d_z, w0, w1, w2, weights, weights, gain_in, *after)


def entry_grad_body(nt_ref, p_ref, o_ref):
    o_ref[...] = dot_nn(nt_ref[...], p_ref[...]).astype(b16)


def entry_grad(normed_t, piece):
    rows, width = piece.shape
    return pl.pallas_call(
        entry_grad_body,
        grid=(width // CB,),
        in_specs=[whole_spec(normed_t.shape), pl.BlockSpec((rows, CB), lambda j: (0, j))],
        out_specs=pl.BlockSpec((D, CB), lambda j: (0, j)),
        out_shape=jax.ShapeDtypeStruct((D, width), b16),
        name="entry_grad",
    )(normed_t, piece)


def group_grad_body(nt_ref, dm_ref, da_ref, o_ref):
    j = pl.program_id(0)
    n_x = GX // CB

    def put(piece):
        o_ref[...] = dot_nn(nt_ref[...], piece).astype(b16)

    @pl.when(j < n_x)
    def _():
        put(dm_ref[0, :, pl.ds(pl.multiple_of(jnp.minimum(j, n_x - 1) * CB, CB), CB)])

    @pl.when(j == n_x)
    def _():
        put(da_ref[0, :, :CB])

    @pl.when(j > n_x)
    def _():
        put(jnp.concatenate([da_ref[0, :, CB:], dm_ref[0, :, GX : GX + 128]], axis=1))


def group_grad(normed_t, d_mix, d_att, g):
    rows = normed_t.shape[1]
    return pl.pallas_call(
        group_grad_body,
        grid=(GCOLS // CB,),
        in_specs=[
            whole_spec(normed_t.shape),
            pl.BlockSpec((1, rows, d_mix.shape[2]), lambda j: (g, 0, 0)),
            pl.BlockSpec((1, rows, d_att.shape[2]), lambda j: (g, 0, 0)),
        ],
        out_specs=pl.BlockSpec((D, CB), lambda j: (0, j)),
        out_shape=jax.ShapeDtypeStruct((D, GCOLS), b16),
        name="group_grad",
    )(normed_t, d_mix, d_att)


def state_grad_body(nt_ref, dm_ref, o_ref):
    o_ref[...] = dot_nn(nt_ref[...], low_sum(dm_ref)).astype(b16)


def state_grad(normed_t, d_mix):
    return pl.pallas_call(
        state_grad_body,
        grid=(1,),
        in_specs=[whole_spec(normed_t.shape), whole_spec(d_mix.shape)],
        out_specs=whole_spec((D, BCW)),
        out_shape=jax.ShapeDtypeStruct((D, BCW), b16),
        name="state_grad",
    )(normed_t, d_mix)


def bit_orders(count):
    bits = list(range(count))
    return [bits[k % count :] + bits[: k % count] for k in (0, 2, 1)]


def partners(size, bit):
    return [(i, i ^ (1 << bit)) for i in range(size)]


def gather_rows(shard, order, size, f_pos, s_pos):
    have = []
    value = shard
    for bit in reversed(order):
        got = lax.ppermute(value, "fsdp", partners(size, bit))
        mine = ((f_pos >> bit) & 1) == 0
        axis = sum(1 for other in have if other > bit)
        value = jnp.stack([jnp.where(mine, value, got), jnp.where(mine, got, value)], axis=axis)
        have.append(bit)
    got = lax.ppermute(value, "seq", SWAP)
    mine = s_pos == 0
    value = jnp.stack(
        [jnp.where(mine, value, got), jnp.where(mine, got, value)], axis=len(have)
    )
    return value.reshape(-1, shard.shape[-1])


def scatter_rows(grad, order, size, f_pos, s_pos):
    rows = grad.shape[0] // (2 * size)
    width = grad.shape[1]
    value = grad.reshape(size, 2, rows, width)
    keep = lax.dynamic_index_in_dim(value, s_pos, 1, keepdims=False)
    send = lax.dynamic_index_in_dim(value, 1 - s_pos, 1, keepdims=False)
    got = lax.ppermute(send, "seq", SWAP)
    value = (keep.astype(f32) + got.astype(f32)).astype(b16)
    have = sorted(order, reverse=True)
    value = value.reshape((2,) * len(have) + (rows, width))
    for step, bit in enumerate(order):
        axis = have.index(bit)
        mine = (f_pos >> bit) & 1
        keep = lax.dynamic_index_in_dim(value, mine, axis, keepdims=False)
        send = lax.dynamic_index_in_dim(value, 1 - mine, axis, keepdims=False)
        got = lax.ppermute(send, "fsdp", partners(size, bit))
        value = keep.astype(f32) + got.astype(f32)
        if step + 1 < len(order):
            value = value.astype(b16)
        have.pop(axis)
    return value


def butterfly(value, size):
    value = value + lax.ppermute(value, "seq", SWAP)
    bit = 0
    while (1 << bit) < size:
        value = value + lax.ppermute(value, "fsdp", partners(size, bit))
        bit += 1
    return value


def exchange(value, s_pos):
    own = lax.dynamic_index_in_dim(value, s_pos, 0, keepdims=False)
    send = lax.dynamic_index_in_dim(value, 1 - s_pos, 0, keepdims=False)
    got = lax.ppermute(send, "seq", SWAP)
    mine = s_pos == 0
    return jnp.stack([jnp.where(mine, own, got), jnp.where(mine, got, own)])


def adam_update(master, moment_one, second, gradient, factor):
    clipped = gradient * factor
    new_one = beta_first * moment_one + (1.0 - beta_first) * clipped
    new_second = beta_second * second + (1.0 - beta_second) * clipped * clipped
    one_hat = new_one / (1.0 - beta_first**STEP)
    second_hat = new_second / (1.0 - beta_second**STEP)
    new_master = master - learn_rate * (
        one_hat / (jnp.sqrt(second_hat) + adam_eps) + decay_rate * master
    )
    return (new_master, new_one, new_second)


def per_device(
    tokens,
    cotangent,
    lengths,
    master_in,
    master_qkv,
    master_ssm_out,
    master_att_out,
    master_gu,
    master_down,
    master_small,
    *state,
):
    moments = state[:7]
    squares = state[7:]
    f_size = lax.axis_size("fsdp")
    f_pos = lax.axis_index("fsdp")
    s_pos = lax.axis_index("seq")
    devices = 2 * f_size
    tok_rows = tokens.shape[0]
    length = 2 * tok_rows
    per_group = NHM // 2
    bits = f_size.bit_length() - 1
    orders = bit_orders(bits)

    def cut(array, first, width):
        return array[:, first : first + width].astype(b16)

    own_rows = master_in.shape[0]
    fill = jnp.zeros((own_rows, 128 - per_group), b16)
    shards = []
    for g in range(2):
        shards.append(
            jnp.concatenate(
                [
                    cut(master_in, DSSM + GX * g, GX),
                    cut(master_qkv, GQ * g, GQ),
                    cut(master_qkv, HQ * HD + HD * g, HD),
                    cut(master_qkv, (HQ + HK) * HD + HD * g, HD),
                    cut(master_in, 2 * DSSM + BCW + per_group * g, per_group),
                    fill,
                ],
                axis=1,
            )
        )
    shards.append(cut(master_in, 2 * DSSM, BCW))
    mid_rows = (
        master_ssm_out.shape[0], master_att_out.shape[0], master_down.shape[0],
        own_rows, own_rows, own_rows, own_rows, own_rows, own_rows // 2,
    )
    half_rows = own_rows // 2
    half = D // 2
    mid_shard = jnp.concatenate(
        [master_ssm_out.astype(b16), master_att_out.astype(b16), master_down.astype(b16)]
        + [cut(master_gu, D * b, D) for b in range(4)]
        + [
            cut(master_in, 0, D),
            jnp.concatenate(
                [cut(master_in[:half_rows], D, half), cut(master_in[half_rows:], D, half)], axis=1
            ),
        ],
        axis=0,
    )
    w_mid = lax.all_gather(mid_shard, BOTH, axis=0, tiled=True).reshape(devices, sum(mid_rows), D)
    w0, w1, w2 = [gather_rows(shards[i], orders[i], f_size, f_pos, s_pos) for i in range(3)]
    if devices != PSEUDO:
        pieces = []
        first = 0
        for rows in mid_rows:
            pieces.append(w_mid[:, first : first + rows].reshape(PSEUDO, -1, D))
            first = first + rows
        folded = pieces.pop().reshape(devices, half_rows, 2, half).transpose(0, 2, 1, 3)
        folded = folded.reshape(PSEUDO, 2, -1, half).transpose(0, 2, 1, 3).reshape(PSEUDO, -1, D)
        w_mid = jnp.concatenate(pieces + [folded], axis=1)

    gain_in, gain_ff, gain_ssm, conv_bias, conv_weight, dt_bias, a_log, d_skip = split_small(
        master_small
    )
    slot_positions = s_pos * tok_rows + jnp.arange(tok_rows, dtype=jnp.int32)
    keep = (slot_positions < lengths[0]).astype(f32)[:, None]
    x_value = tokens.astype(f32)
    normed = (x_value * rms_scale(x_value) * gain_in).astype(b16)
    normed_t = normed.T
    cos, sin = rope_rows(length)
    rot = turn_matrix()
    seg = (
        lax.broadcasted_iota(jnp.int32, (GX, 128), 0) // HDM
        == lax.broadcasted_iota(jnp.int32, (GX, 128), 1)
    ).astype(b16)
    x_offset = s_pos * GX
    head_offset = s_pos * per_group
    conv_cols = jnp.concatenate(
        [lax.dynamic_slice_in_dim(conv_weight, x_offset, GX, 1), conv_weight[:, DSSM:]], axis=1
    )
    conv_rows = jnp.concatenate([conv_cols, jnp.zeros((8 - KCONV, GX + BCW), f32)], axis=0)
    bias_row = jnp.concatenate(
        [lax.dynamic_slice_in_dim(conv_bias, x_offset, GX, 0), conv_bias[DSSM:]]
    )[None]
    heads = lambda v: lax.dynamic_slice_in_dim(v, head_offset, per_group, 0)
    wide = lambda v: jnp.pad(v, (0, 128 - per_group))
    head_rows = jnp.pad(
        jnp.stack([wide(heads(dt_bias)), wide(-jnp.exp(heads(a_log)))]), ((0, 6), (0, 0))
    )
    skip_row = jnp.repeat(heads(d_skip), HDM)[None]

    mixed = exchange(project_send(normed, w0, w1, w2), s_pos).reshape(length, GCOLS + BCW)
    z_gate = project_gate(normed, w_mid)
    att_out, lse = attn_fwd(mixed, cos, sin, rot, GQ)
    att_back = exchange(att_out.reshape(2, tok_rows, GQ), s_pos)
    y_out, states = mamba_fwd(mixed, conv_rows, bias_row, head_rows, skip_row, GX)
    ys_back = exchange(y_out.reshape(2, tok_rows, GX), s_pos)
    (
        output, d_residual, ssm_norm, ff_in, hidden, d_gate_up, d_branch, d_mixer, d_ys, d_att, d_z,
        grad_gain_ff, grad_gain_ssm,
    ) = middle(
        tokens, cotangent, keep, ys_back, att_back, z_gate, w_mid, gain_ff[None], gain_ssm[None]
    )
    mid_grads = middle_grads(ff_in, hidden, ssm_norm, att_back, d_gate_up, d_branch, d_mixer)
    if devices != PSEUDO:
        pieces = []
        first = 0
        for rows in mid_rows[:7]:
            rows = rows * devices // PSEUDO
            pieces.append(mid_grads[:, first : first + rows].reshape(devices, -1, D))
            first = first + rows
        mid_grads = jnp.concatenate(pieces, axis=1)
    mid_owned = lax.psum_scatter(
        mid_grads.reshape(-1, D), BOTH, scatter_dimension=0, tiled=True
    ).astype(f32)
    gate_grad = entry_grad(normed_t, d_z)
    o3 = scatter_rows(gate_grad, orders[1], f_size, f_pos, s_pos)
    d_att_rows = exchange(d_att, s_pos).reshape(length, GQ)
    d_y_rows = exchange(d_ys, s_pos).reshape(length, GX)
    att_grads = attn_bwd(mixed, cos, sin, rot, lse, d_att_rows)
    att_grads = exchange(att_grads.reshape(2, tok_rows, -1), s_pos)
    mix_grads, conv_grads, head_grads, skip_grads = mamba_bwd(
        mixed, d_y_rows, states, conv_rows, bias_row, head_rows, skip_row, seg, gate_grad, GX
    )
    mix_grads = exchange(mix_grads.reshape(2, tok_rows, -1), s_pos)
    late = (
        group_grad(normed_t, mix_grads, att_grads, 0),
        group_grad(normed_t, mix_grads, att_grads, 1),
        state_grad(normed_t, mix_grads),
    )
    o0, o1, o2 = [
        scatter_rows(piece, orders[i], f_size, f_pos, s_pos) for i, piece in enumerate(late)
    ]
    token_grad, grad_gain_in = entry_back(
        tokens, d_residual, mix_grads, att_grads, d_z, w0, w1, w2, w_mid, gain_in[None], late
    )
    grad_in = jnp.concatenate(
        [
            o3, o0[:, :GX], o1[:, :GX], o2,
            o0[:, GDT : GDT + per_group], o1[:, GDT : GDT + per_group],
        ],
        axis=1,
    )
    grad_qkv = jnp.concatenate(
        [
            o0[:, GX : GX + GQ], o1[:, GX : GX + GQ],
            o0[:, GX + GQ : GX + GQ + HD], o1[:, GX + GQ : GX + GQ + HD],
            o0[:, GX + GQ + HD : GDT], o1[:, GX + GQ + HD : GDT],
        ],
        axis=1,
    )
    mid_pieces = []
    first = 0
    for rows in mid_rows[:7]:
        mid_pieces.append(mid_owned[first : first + rows])
        first = first + rows
    grad_gu = jnp.concatenate(mid_pieces[3:], axis=1)
    owned = (grad_in, grad_qkv, mid_pieces[0], mid_pieces[1], grad_gu, mid_pieces[2])

    conv_bias_grad = jnp.concatenate(
        [
            lax.dynamic_update_slice_in_dim(
                jnp.zeros((DSSM,), f32), conv_grads[KCONV, :GX], x_offset, 0
            ),
            conv_grads[KCONV, GX:],
        ]
    )
    conv_weight_grad = jnp.concatenate(
        [
            lax.dynamic_update_slice_in_dim(
                jnp.zeros((KCONV, DSSM), f32), conv_grads[:KCONV, :GX], x_offset, 1
            ),
            conv_grads[:KCONV, GX:],
        ],
        axis=1,
    )
    head_zeros = jnp.zeros((NHM,), f32)
    place = lambda v: lax.dynamic_update_slice_in_dim(head_zeros, v, head_offset, 0)
    small_local = jnp.concatenate(
        [
            grad_gain_in[0],
            grad_gain_ff[0],
            grad_gain_ssm[0],
            conv_bias_grad,
            conv_weight_grad.reshape(KCONV * CONVW),
            place(head_grads[0, :per_group]),
            place(head_grads[1, :per_group]),
            place(jnp.sum(skip_grads[0].reshape(per_group, HDM), axis=1)),
        ]
    )
    n_small = small_local.shape[0]
    small_rows = jnp.pad(small_local, (0, -n_small % 1024)).reshape(-1, 128)
    small_total = butterfly(small_rows, f_size).reshape(-1)[:n_small]
    local_square = jnp.zeros((), f32)
    for g in owned:
        local_square = local_square + jnp.sum(g * g)
    square_total = butterfly(jnp.broadcast_to(local_square, (8, 128)), f_size)[0, 0] + jnp.sum(
        small_total * small_total
    )
    grad_norm = jnp.sqrt(square_total)
    factor = jnp.minimum(1.0, clip_norm / (grad_norm + 1e-06))
    all_grads = owned + (small_total,)
    masters = (
        master_in,
        master_qkv,
        master_ssm_out,
        master_att_out,
        master_gu,
        master_down,
        master_small,
    )
    updated = [
        adam_update(masters[i], moments[i], squares[i], all_grads[i], factor) for i in range(7)
    ]
    return (
        (output, token_grad, grad_norm)
        + all_grads
        + tuple(updated[i][0] for i in range(6))
        + (updated[6][0] - master_small,)
        + tuple(updated[i][1] for i in range(7))
        + tuple(updated[i][2] for i in range(7))
    )


def solution(mesh):
    rows = P(BOTH, None)
    weights = (rows,) * 6 + (P(),)
    return jax.shard_map(
        per_device,
        mesh=mesh,
        in_specs=(rows, rows, P("fsdp")) + weights * 3,
        out_specs=(rows, rows, P()) + weights * 4,
        check_vma=False,
    )
```
